32 devices in a mesh: row: 8 (over y, x, core), col: 4 (over z).
Axes of the slice: x: 2, y: 2, z: 4, core: 2. Of those that a mesh axis runs over, the one named last changes fastest.
Arguments:
- features: bfloat16 [512, 16384], P('col', 'row'), may hold values from -6 to 6
- weight: bfloat16 [512, 512], replicated, may hold values from -0.25 to 0.25
- tile_cols: int32 [8, 256], P('row'), may hold values from 0 to 127, as said below
- tile_rows: int32 [8, 256], P('row'), may hold values from 0 to 15
- tile_count: int32 [8], P('row'), may hold values from 1 to 256, as said below
- tile_values: bfloat16 [2048, 128, 128], P('row'), may hold values from 0 to 0.049804688
- out_grad: bfloat16 [512, 16384], P('col', 'row'), may hold values from -6 to 6
Outputs:
- output: bfloat16 [512, 16384], P('col', 'row')
- input_grad: bfloat16 [512, 16384], P('col', 'row')
- weight_grad: float32 [512, 512], P(None, 'col')
The draws below stay inside these ranges and needn't reach their ends.
Inputs may be any that keep to these rules, and one draw needn't show every extreme that they name: `tile_cols`: the column tiles used by the slots t < tile_count[r] of row index r that lie in the range of one other row index s (tiles s * 16 to s * 16 + 15) are at most 4 distinct ones, and some pair r, s has exactly 4. Slots past tile_count[r] hold in-range entries that are not used. `tile_count`: some row index uses all 256 slots.
All inputs are finite; a program needn't handle non-finite values.
Results may differ from the reference program's by a relative error of at most 0.0061.
Values may be sent and summed in bfloat16 or wider, within the bound.
No kernel may reach another device: no remote copies, remote signals or barrier semaphores. Data moves between devices by JAX's collectives and lax.ppermute only.
A program may use at most 128 MiB of HBM per device.

```python
import jax
import jax.numpy as jnp
from jax import lax

F = 512
H = 512
TILE = 128
MAXT = 256
TROWS = 16
SLOT = 4
NODES = 16384
BLOCKS = 128
N_ROW = 8


def tile_layout(key):
    keys = jax.random.split(jax.random.fold_in(key, 11), 8)
    lowest = max(MAXT // 8, 1)
    counts = jax.random.randint(keys[0], (N_ROW,), lowest, MAXT // 2 + 1)
    fullest = jax.random.randint(keys[1], (), 0, N_ROW)
    device = jnp.arange(N_ROW, dtype=jnp.int32)
    counts = jnp.where(device == fullest, MAXT, counts)
    row_ids = jax.random.randint(keys[2], (N_ROW, MAXT), 0, TROWS)
    remote = jax.random.randint(keys[3], (N_ROW, MAXT), 0, 2) == 1
    other = (device[:, None] + 1 + jax.random.randint(keys[4], (N_ROW, MAXT), 0, N_ROW - 1)) % N_ROW
    offsets = jax.random.randint(keys[5], (N_ROW, N_ROW), 0, TROWS)
    stepping = jax.random.randint(keys[6], (N_ROW, MAXT), 0, SLOT)
    nearby = jax.random.randint(keys[7], (N_ROW, MAXT), 0, TROWS)
    slot_ids = jnp.arange(MAXT, dtype=jnp.int32)[None, :]
    forced = (device[:, None] == fullest) & (slot_ids < SLOT)
    remote = remote | forced
    other = jnp.where(forced, (fullest + 1) % N_ROW, other)
    stepping = jnp.where(forced, slot_ids, stepping)
    distant = (jnp.take_along_axis(offsets, other, axis=1) + stepping) % TROWS
    col_ids = jnp.where(remote, other * TROWS + distant, device[:, None] * TROWS + nearby)
    return (col_ids.astype(jnp.int32), row_ids.astype(jnp.int32), counts.astype(jnp.int32))


def draw_tile_cols(key, part):
    return tile_layout(key)[0]


def draw_tile_rows(key, part):
    return tile_layout(key)[1]


def draw_tile_count(key, part):
    return tile_layout(key)[2]


def steps_of(rng, extent, cuts, low, largest):
    def one(dim, parts):
        draws = jax.random.uniform(jax.random.fold_in(jax.random.fold_in(rng, 6), dim), (parts,), jnp.float32, low / len(cuts), largest / len(cuts))
        return jnp.repeat(jnp.exp(draws), extent[dim] // parts).reshape((-1,) + (1,) * (len(extent) - dim - 1))

    factor_of = one(*cuts[0])
    for cut in cuts[1:]:
        factor_of = factor_of * one(*cut)
    return factor_of


def bell_draw(own_key, extent, width, limit, cuts=(), held_as=jnp.bfloat16):
    loudness = steps_of(own_key, extent, cuts, -0.22, 0.18) if cuts else 1.0
    drawn = jax.random.normal(own_key, extent, jnp.float32) * width * loudness
    return jnp.minimum(jnp.maximum(drawn, -limit), limit).astype(held_as)


def setup_inputs(seed: int = 0) -> dict:
    arg_keys = jax.random.split(jax.random.key(seed), 8)
    return {
        "features": bell_draw(arg_keys[0], (F, NODES), 1.0, 6.0, ((0, 4), (1, 8))),
        "weight": bell_draw(arg_keys[1], (F, H), F ** -0.5, 0.25),
        "tile_cols": draw_tile_cols(jax.random.fold_in(arg_keys[7], 71), 0),
        "tile_rows": draw_tile_rows(jax.random.fold_in(arg_keys[7], 71), 0),
        "tile_count": draw_tile_count(jax.random.fold_in(arg_keys[7], 71), 0),
        "tile_values": jnp.clip(0.049804688 * jax.random.uniform(arg_keys[5], (N_ROW * MAXT, TILE, TILE), jnp.float32) ** steps_of(arg_keys[5], (N_ROW * MAXT, TILE, TILE), ((0, 8),), -0.2, 0.2), 0.0, 0.049804688).astype(jnp.bfloat16),
        "out_grad": bell_draw(arg_keys[6], (H, NODES), 1.0, 6.0, ((0, 4), (1, 8))),
    }


def reference(features, weight, tile_cols, tile_rows, tile_count, tile_values, out_grad):
    projected = jnp.dot(weight.T, features, preferred_element_type=jnp.float32).astype(jnp.bfloat16)
    proj_blocks = projected.reshape(H, BLOCKS, TILE)
    values = tile_values.reshape(N_ROW, MAXT, TILE, TILE)
    slot_ids = jnp.arange(MAXT, dtype=jnp.int32)
    row_span = jnp.arange(TROWS, dtype=jnp.int32)

    def forward_rows(item):
        col_ids, row_ids, count_one, tiles = item
        in_use = (slot_ids < count_one).astype(jnp.float32)
        picked = jnp.take(proj_blocks, col_ids, axis=1).astype(jnp.float32)
        products = jnp.einsum("htm,tnm->thn", picked, tiles.astype(jnp.float32), precision=lax.Precision.HIGHEST)
        placing = (row_ids[:, None] == row_span[None, :]).astype(jnp.float32) * in_use[:, None]
        return jnp.einsum("ti,thn->hin", placing, products, precision=lax.Precision.HIGHEST)

    preact = lax.map(forward_rows, (tile_cols, tile_rows, tile_count, values))
    preact = preact.transpose(1, 0, 2, 3).reshape(H, NODES)
    logistic = jax.nn.sigmoid(preact)
    output = (preact * logistic).astype(jnp.bfloat16)
    slope_v = logistic * (1.0 + preact * (1.0 - logistic))
    z_grad = (out_grad.astype(jnp.float32) * slope_v).astype(jnp.bfloat16)
    z_dev = z_grad.reshape(H, N_ROW, TROWS, TILE).transpose(1, 0, 2, 3)

    def backward_rows(carry, item):
        col_ids, row_ids, count_one, tiles, z_rows = item
        in_use = (slot_ids < count_one).astype(jnp.float32)
        picked = jnp.take(z_rows, row_ids, axis=1).astype(jnp.float32)
        products = jnp.einsum("htn,tnm->thm", picked, tiles.astype(jnp.float32), precision=lax.Precision.HIGHEST)
        products = products * in_use[:, None, None]
        return carry + jax.ops.segment_sum(products, col_ids, num_segments=BLOCKS), None

    start_sum = jnp.zeros((BLOCKS, H, TILE), jnp.float32)
    p_sum, _ = lax.scan(backward_rows, start_sum, (tile_cols, tile_rows, tile_count, values, z_dev))
    p_grad = p_sum.transpose(1, 0, 2).reshape(H, NODES).astype(jnp.bfloat16)
    input_grad = jnp.dot(weight, p_grad, preferred_element_type=jnp.float32).astype(jnp.bfloat16)
    weight_grad = jnp.dot(features, p_grad.T, preferred_element_type=jnp.float32) * (NODES ** -0.5)
    return output, input_grad, weight_grad
```

```python
import functools

import jax
import jax.numpy as jnp
from jax import lax
from jax.experimental import pallas as pl
from jax.experimental.pallas import tpu as pltpu
from jax.sharding import PartitionSpec as P

TILE = 128
SLOT = 4
UNROLL = 4
BF = jnp.bfloat16
F32 = jnp.float32
VM = pl.BlockSpec(memory_space=pltpu.VMEM)
SM = pl.BlockSpec(memory_space=pltpu.SMEM)


def call(kernel, outs, scratch, smem, vmem, flops=0, nbytes=0, limit=32):
    return pl.pallas_call(
        kernel,
        out_shape=outs,
        in_specs=[SM] * len(smem) + [VM] * len(vmem),
        out_specs=jax.tree.map(lambda _: VM, outs),
        scratch_shapes=scratch,
        compiler_params=pltpu.CompilerParams(vmem_limit_bytes=limit << 20),
        cost_estimate=pl.CostEstimate(flops=flops, bytes_accessed=nbytes, transcendentals=0),
    )(*smem, *vmem)


def swap(x, axis, n, k):
    return lax.ppermute(x, axis, [(i, i ^ k) for i in range(n)])


def tile_list(key, valid, groups, source, blank):
    slots = key.shape[0]
    ids = jnp.arange(slots, dtype=jnp.int32)
    gids = jnp.arange(groups, dtype=jnp.int32)
    key = jnp.where(valid, key, -1)
    count = jnp.sum((key[None, :] == gids[:, None]).astype(jnp.int32), axis=1)
    even = (count + 1) & ~1
    start = jnp.sum(jnp.where(gids[None, :] < gids[:, None], even[None, :], 0), axis=1)
    rank = jnp.sum(
        ((key[None, :] == key[:, None]) & (ids[None, :] < ids[:, None])).astype(jnp.int32), axis=1
    )
    first = jnp.sum(jnp.where(key[:, None] == gids[None, :], start[None, :], 0), axis=1)
    place = jnp.where(valid, first + rank, -1)
    word = ids | (source << 10) | (key << 20)
    pad = blank << 10
    length = -(-(slots + groups) // (2 * UNROLL)) * 2 * UNROLL
    places = jnp.arange(length, dtype=jnp.int32)
    hit = places[:, None] == place[None, :]
    words = jnp.sum(jnp.where(hit, word[None, :] - pad, 0), axis=1) + pad
    pairs = jnp.sum(even) // 2
    return words, ((pairs + UNROLL - 1) // UNROLL).reshape(1)


def sparse_loop(list_ref, steps_ref, x_ref, tiles_ref, acc_ref, forward):
    def step(s, carry):
        for u in range(UNROLL):
            w0 = list_ref[(s * UNROLL + u) * 2]
            w1 = list_ref[(s * UNROLL + u) * 2 + 1]
            x = jnp.concatenate([x_ref[(w0 >> 10) & 1023], x_ref[(w1 >> 10) & 1023]], axis=1)
            t0, t1 = tiles_ref[w0 & 1023], tiles_ref[w1 & 1023]
            if forward:
                part = lax.dot_general(
                    x,
                    jnp.concatenate([t0, t1], axis=1),
                    (((1,), (1,)), ((), ())),
                    preferred_element_type=F32,
                )
            else:
                part = jnp.dot(x, jnp.concatenate([t0, t1], axis=0), preferred_element_type=F32)
            acc_ref[w0 >> 20] += part
        return carry

    lax.fori_loop(0, steps_ref[0], step, 0)


def send_kernel(peers, want_ref, me_ref, feat_ref, *out_refs):
    for d, out in enumerate(out_refs):
        peer = me_ref[0] ^ (d + 1)
        for j in range(SLOT):
            col = pl.multiple_of(want_ref[peer * SLOT + j] * TILE, TILE)
            out[j] = feat_ref[:, pl.ds(col, TILE)]


def fill_from_wide(x_ref, wide_ref, count):
    for k in range(count):
        x_ref[k] = wide_ref[:, k * TILE : (k + 1) * TILE]
    x_ref[count] = jnp.zeros_like(x_ref[count])


def local_kernel(forward, list_ref, steps_ref, wide_ref, tiles_ref, acc_ref, x_ref):
    fill_from_wide(x_ref, wide_ref, x_ref.shape[0] - 1)
    acc_ref[...] = jnp.zeros_like(acc_ref)
    sparse_loop(list_ref, steps_ref, x_ref, tiles_ref, acc_ref, forward)


def remote_fwd_kernel(n_in, list_ref, steps_ref, me_ref, *refs):
    ins, (tiles_ref, base_ref), rest = refs[:n_in], refs[n_in : n_in + 2], refs[n_in + 2 :]
    outs, (x_ref, acc_ref) = rest[:-2], rest[-2:]
    for d, r in enumerate(ins):
        x_ref[d * SLOT : (d + 1) * SLOT] = r[...]
    x_ref[n_in * SLOT] = jnp.zeros_like(x_ref[0])
    acc_ref[...] = base_ref[...]
    sparse_loop(list_ref, steps_ref, x_ref, tiles_ref, acc_ref, True)
    per = acc_ref.shape[0] // len(outs)
    for k, out in enumerate(outs):
        block = me_ref[0] ^ k
        for i in range(per):
            out[:, i * TILE : (i + 1) * TILE] = acc_ref[block * per + i].astype(BF)


def dense_kernel(n_col, me_ref, wt_ref, w_ref, *refs):
    s_refs, g_refs = refs[:n_col], refs[n_col : 2 * n_col]
    o_refs, y_refs = refs[2 * n_col : 3 * n_col], refs[3 * n_col : 4 * n_col]
    z_ref, s_ref = refs[4 * n_col], refs[4 * n_col + 1]
    f_loc = s_refs[0].shape[0]
    me = me_ref[0]
    for k in range(n_col):
        s_ref[pl.ds(pl.multiple_of((me ^ k) * f_loc, f_loc), f_loc), :] = s_refs[k][...]
    s_all = s_ref[...]
    for k in range(n_col):
        rows = pl.ds(pl.multiple_of((me ^ k) * f_loc, f_loc), f_loc)
        pre = jnp.dot(wt_ref[rows, :], s_all, preferred_element_type=F32)
        sig = 1.0 / (1.0 + jnp.exp(-pre))
        o_refs[k][...] = (pre * sig).astype(BF)
        slope = sig * (1.0 + pre * (1.0 - sig))
        z_ref[rows, :] = (g_refs[k][...].astype(F32) * slope).astype(BF)
    z_all = z_ref[...]
    for k in range(n_col):
        rows = pl.ds(pl.multiple_of((me ^ k) * f_loc, f_loc), f_loc)
        y_refs[k][...] = jnp.dot(w_ref[rows, :], z_all, preferred_element_type=F32).astype(BF)


def weight_kernel(me_ref, s_ref, z_ref, own_ref, *outs):
    per = own_ref.shape[0]
    z = z_ref[...]
    for d in range(len(outs) + 1):
        rows = pl.ds(pl.multiple_of((me_ref[0] ^ d) * per, per), per)
        part = lax.dot_general(
            s_ref[rows, :], z, (((1,), (1,)), ((), ())), preferred_element_type=F32
        )
        if d == 0:
            own_ref[...] = part
        else:
            outs[d - 1][...] = part.astype(BF)


def gather_blocks(wide_ref, me, refs):
    width = refs[0].shape[1]
    for k, r in enumerate(refs):
        wide_ref[:, pl.ds(pl.multiple_of((me ^ k) * width, width), width)] = r[...]


def remote_bwd_kernel(n_col, list_ref, steps_ref, me_ref, *refs):
    ins, tiles_ref, rest = refs[:n_col], refs[n_col], refs[n_col + 1 :]
    wide_ref, (x_ref, acc_ref) = rest[0], rest[-2:]
    outs = rest[1:-2]
    gather_blocks(wide_ref, me_ref[0], ins)
    fill_from_wide(x_ref, wide_ref, x_ref.shape[0] - 1)
    acc_ref[...] = jnp.zeros_like(acc_ref)
    sparse_loop(list_ref, steps_ref, x_ref, tiles_ref, acc_ref, False)
    for d, out in enumerate(outs):
        out[...] = acc_ref[d * SLOT : (d + 1) * SLOT].astype(BF)


def join_kernel(want_ref, me_ref, base_ref, *refs):
    ins, out_ref, acc_ref = refs[:-2], refs[-2], refs[-1]
    acc_ref[...] = base_ref[...]
    for d, r in enumerate(ins):
        peer = me_ref[0] ^ (d + 1)
        for j in range(SLOT):
            acc_ref[want_ref[peer * SLOT + j]] += r[j].astype(F32)
    for k in range(acc_ref.shape[0]):
        out_ref[:, k * TILE : (k + 1) * TILE] = acc_ref[k].astype(BF)


def place_kernel(me_ref, *refs):
    gather_blocks(refs[-1], me_ref[0], refs[:-1])


def shards(features, weight, tile_cols, tile_rows, tile_count, tile_values, out_grad):
    n_row, n_col = lax.axis_size("row"), lax.axis_size("col")
    me_r, me_c = lax.axis_index("row").astype(jnp.int32), lax.axis_index("col").astype(jnp.int32)
    mer, mec = me_r.reshape(1), me_c.reshape(1)
    f_loc, nodes = features.shape
    h_loc = out_grad.shape[0]
    n_f, n_h = weight.shape
    row_tiles = nodes // TILE
    part = nodes // n_col
    slots = tile_cols.shape[1]
    cols, rows = tile_cols[0], tile_rows[0]
    valid = jnp.arange(slots, dtype=jnp.int32) < tile_count[0]

    blocks = jnp.arange(n_row * row_tiles, dtype=jnp.int32)
    seen = jnp.any((cols[None, :] == blocks[:, None]) & valid[None, :], axis=1)
    seen = seen.reshape(n_row, row_tiles)
    inner = jnp.arange(row_tiles, dtype=jnp.int32)
    below = inner[None, :] < inner[:, None]
    rank = jnp.sum((seen[:, None, :] & below[None]).astype(jnp.int32), axis=2)
    slot_ids = jnp.arange(SLOT, dtype=jnp.int32)
    chosen = seen[:, None, :] & (rank[:, None, :] == slot_ids[None, :, None])
    need = jnp.sum(jnp.where(chosen, inner[None, None, :], 0), axis=2)
    want = lax.all_to_all(need, "row", 0, 0, tiled=True).reshape(n_row * SLOT)

    owner, inside = cols // row_tiles, cols % row_tiles
    slot_of = jnp.sum(
        jnp.where(cols[:, None] == blocks[None, :], rank.reshape(-1)[None, :], 0), axis=1
    )
    away = ((owner ^ me_r) - 1) * SLOT + slot_of
    mine, far = valid & (owner == me_r), valid & (owner != me_r)
    n_away = (n_row - 1) * SLOT
    list_fl, steps_fl = tile_list(rows, mine, row_tiles, inside, row_tiles)
    list_fr, steps_fr = tile_list(rows, far, row_tiles, away, n_away)
    list_br, steps_br = tile_list(away, far, n_away, rows, row_tiles)
    list_bl, steps_bl = tile_list(inside, mine, row_tiles, rows, row_tiles)

    block = (SLOT, f_loc, TILE)
    sds = jax.ShapeDtypeStruct
    tile_flops = 2 * f_loc * TILE * TILE
    tile_bytes = slots * TILE * TILE * 2

    sends = call(
        functools.partial(send_kernel, n_row - 1),
        [sds(block, BF)] * (n_row - 1),
        [],
        (want, mer),
        (features,),
        nbytes=2 * n_away * f_loc * TILE * 2,
    )
    got = [swap(x, "row", n_row, d + 1) for d, x in enumerate(sends)]

    def split_cols(x):
        return [lax.dynamic_slice_in_dim(x, (me_c ^ k) * part, part, 1) for k in range(n_col)]

    grads = [g if k == 0 else swap(g, "col", n_col, k) for k, g in enumerate(split_cols(out_grad))]

    acc = call(
        functools.partial(local_kernel, True),
        sds((row_tiles, f_loc, TILE), F32),
        [pltpu.VMEM((row_tiles + 1, f_loc, TILE), BF)],
        (list_fl, steps_fl),
        (features, tile_values),
        flops=tile_flops * slots,
        nbytes=tile_bytes,
    )
    s_parts = call(
        functools.partial(remote_fwd_kernel, n_row - 1),
        [sds((f_loc, part), BF)] * n_col,
        [pltpu.VMEM((n_away + 1, f_loc, TILE), BF), pltpu.VMEM((row_tiles, f_loc, TILE), F32)],
        (list_fr, steps_fr, mec),
        (*got, tile_values, acc),
        flops=tile_flops * slots,
        nbytes=tile_bytes,
    )
    s_got = [s if k == 0 else swap(s, "col", n_col, k) for k, s in enumerate(s_parts)]

    res = call(
        functools.partial(dense_kernel, n_col),
        [sds((h_loc, part), BF)] * n_col
        + [sds((f_loc, part), BF)] * n_col
        + [sds((n_h, part), BF), sds((n_f, part), BF)],
        [],
        (mec,),
        (weight.T, weight, *s_got, *grads),
        flops=4 * n_f * n_h * part,
        nbytes=n_f * part * 8,
    )
    o_parts, y_parts, z_all, s_all = res[:n_col], res[n_col : 2 * n_col], res[-2], res[-1]
    y_got = [y if k == 0 else swap(y, "col", n_col, k) for k, y in enumerate(y_parts)]

    w_rows = n_f // n_row
    w_parts = call(
        weight_kernel,
        [sds((w_rows, n_h), F32)] + [sds((w_rows, n_h), BF)] * (n_row - 1),
        [],
        (mer,),
        (s_all, z_all),
        flops=2 * n_f * n_h * part,
        nbytes=n_f * part * 8,
    )
    w_sum = w_parts[0]
    for d in range(1, n_row):
        w_sum = w_sum + swap(w_parts[d], "row", n_row, d).astype(F32)

    back = call(
        functools.partial(remote_bwd_kernel, n_col),
        [sds((f_loc, nodes), BF)] + [sds(block, BF)] * (n_row - 1),
        [pltpu.VMEM((row_tiles + 1, f_loc, TILE), BF), pltpu.VMEM((n_away, f_loc, TILE), F32)],
        (list_br, steps_br, mec),
        (*y_got, tile_values),
        flops=tile_flops * slots,
        nbytes=tile_bytes,
    )
    y_wide, contribs = back[0], back[1:]
    returned = [swap(x, "row", n_row, d + 1) for d, x in enumerate(contribs)]

    o_got = [o if k == 0 else swap(o, "col", n_col, k) for k, o in enumerate(o_parts)]
    w_cols = [
        lax.dynamic_slice_in_dim(w_sum, (me_c ^ k) * h_loc, h_loc, 1) for k in range(n_col)
    ]
    w_mine = w_cols[0]
    for k in range(1, n_col):
        w_mine = w_mine + swap(w_cols[k], "col", n_col, k)
    w_mine = w_mine * float(nodes * n_row) ** (-0.5)
    weight_grad = lax.all_gather(w_mine, "row", axis=0, tiled=True)

    acc_b = call(
        functools.partial(local_kernel, False),
        sds((row_tiles, f_loc, TILE), F32),
        [pltpu.VMEM((row_tiles + 1, f_loc, TILE), BF)],
        (list_bl, steps_bl),
        (y_wide, tile_values),
        flops=tile_flops * slots,
        nbytes=tile_bytes,
    )
    input_grad = call(
        join_kernel,
        sds((f_loc, nodes), BF),
        [pltpu.VMEM((row_tiles, f_loc, TILE), F32)],
        (want, mer),
        (acc_b, *returned),
        nbytes=f_loc * nodes * 8,
    )
    output = call(
        place_kernel, sds((h_loc, nodes), BF), [], (mec,), tuple(o_got), nbytes=h_loc * nodes * 4
    )
    return output, input_grad, weight_grad


def solution(mesh):
    return jax.shard_map(
        shards,
        mesh=mesh,
        in_specs=(
            P("col", "row"),
            P(),
            P("row", None),
            P("row", None),
            P("row"),
            P("row", None, None),
            P("col", "row"),
        ),
        out_specs=(P("col", "row"), P("col", "row"), P(None, "col")),
        check_vma=False,
    )
```

```python
import functools

import jax
import jax.numpy as jnp
from jax import lax
from jax.experimental import pallas as pl
from jax.experimental.pallas import tpu as pltpu
from jax.sharding import PartitionSpec as P

TILE = 128
SLOT = 4
UNROLL = 4
LOADS = 8
BF = jnp.bfloat16
F32 = jnp.float32
VM = pl.BlockSpec(memory_space=pltpu.VMEM)
SM = pl.BlockSpec(memory_space=pltpu.SMEM)


def call(kernel, outs, scratch, smem, vmem, held=(), flops=0, nbytes=0, limit=24):
    return pl.pallas_call(
        kernel,
        out_shape=outs,
        in_specs=[SM] * len(smem) + [VM] * len(held) + [VM] * len(vmem),
        out_specs=jax.tree.map(lambda _: VM, outs),
        scratch_shapes=scratch,
        compiler_params=pltpu.CompilerParams(vmem_limit_bytes=limit << 20),
        cost_estimate=pl.CostEstimate(flops=flops, bytes_accessed=nbytes, transcendentals=0),
    )(*[pltpu.with_memory_space_constraint(x, pltpu.SMEM) for x in smem], *held, *vmem)


def swap(x, axis, n, k):
    return lax.ppermute(x, axis, [(i, i ^ k) for i in range(n)])


def flip(x, n):
    i = lax.broadcasted_iota(jnp.int32, (n, n), 0)
    j = lax.broadcasted_iota(jnp.int32, (n, n), 1)
    return jnp.sum(jnp.where(i == j, x, 0), axis=1 if x.shape[0] == 1 else 0, keepdims=True)


def iota(n, axis):
    return lax.broadcasted_iota(jnp.int32, (n, 1) if axis == 0 else (1, n), axis)


def ranks(cols, valid, blocks, row_tiles):
    b_col, b_row = iota(blocks, 0), iota(blocks, 1)
    hit = jnp.where((cols == b_col) & valid, 1, 0)
    used_col = jnp.max(hit, axis=1, keepdims=True)
    used_row = flip(used_col, blocks)
    same = (b_col // row_tiles) == (b_row // row_tiles)
    rank_row = jnp.sum(jnp.where(same & (b_col < b_row), used_col, 0), axis=0, keepdims=True)
    rank_col = jnp.sum(jnp.where(same & (b_row < b_col), used_row, 0), axis=1, keepdims=True)
    return used_row, rank_row, rank_col


def need_kernel(n_row, row_tiles, count_ref, cols_ref, need_ref):
    cols = cols_ref[...]
    blocks = n_row * row_tiles
    valid = iota(cols.shape[1], 1) < count_ref[0]
    used, rank, _ = ranks(cols, valid, blocks, row_tiles)
    b = iota(blocks, 1)
    owner = (b // row_tiles) == iota(n_row, 0)
    lane = iota(128, 1)
    total = jnp.zeros((n_row, 128), jnp.int32)
    for j in range(SLOT):
        pick = jnp.where((used > 0) & (rank == j), b % row_tiles, 0)
        total += jnp.where(
            lane == j, jnp.sum(jnp.where(owner, pick, 0), axis=1, keepdims=True), 0
        )
    need_ref[...] = total


def write_list(out_ref, which, key_row, key_col, valid_row, valid_col, groups, source, blank):
    slots, length = key_row.shape[1], out_ref.shape[1]
    t_row, t_col = iota(slots, 1), iota(slots, 0)
    key_row, key_col = jnp.where(valid_row, key_row, -1), jnp.where(valid_col, key_col, -1)
    g_col, g_row = iota(groups, 0), iota(128, 1)
    count = jnp.sum(jnp.where(key_row == g_col, 1, 0), axis=1, keepdims=True)
    even = ((count + 1) >> 1) << 1
    start = jnp.sum(jnp.where(g_col < g_row, even, 0), axis=0, keepdims=True)
    first = jnp.sum(jnp.where(key_col == g_row, start, 0), axis=1, keepdims=True)
    rank = jnp.sum(jnp.where((key_row == key_col) & (t_row < t_col), 1, 0), axis=1, keepdims=True)
    place = jnp.where(valid_col, first + rank, -1)
    word = t_col | (source << 10) | (key_col << 20)
    pad = blank << 10
    words = jnp.sum(jnp.where(place == iota(length, 1), word - pad, 0), axis=0, keepdims=True) + pad
    out_ref[which : which + 1, :] = words
    total = jnp.sum(even, axis=0, keepdims=True)
    steps = (total + (2 * UNROLL - 1)) // (2 * UNROLL)
    out_ref[4 + which : 5 + which, :] = jnp.broadcast_to(steps, (1, length))


def lists_kernel(n_row, row_tiles, count_ref, me_ref, cols_ref, rows_ref, out_ref):
    cols, rows = cols_ref[...], rows_ref[...]
    slots = cols.shape[1]
    blocks = n_row * row_tiles
    me, n_chip = me_ref[0], n_row // 2
    valid = iota(slots, 1) < count_ref[0]
    _, rank_row, rank_col = ranks(cols, valid, blocks, row_tiles)
    cols_c, rows_c = flip(cols, slots), flip(rows, slots)
    valid_c = iota(slots, 0) < count_ref[0]
    slot_c = jnp.sum(jnp.where(cols_c == iota(blocks, 1), rank_row, 0), axis=1, keepdims=True)
    slot_r = jnp.sum(jnp.where(cols == iota(blocks, 0), rank_col, 0), axis=0, keepdims=True)

    def away(c, s):
        owner = c // row_tiles
        return ((owner >> 1) ^ (me >> 1)) * (2 * SLOT) + (owner & 1) * SLOT + s

    away_r, away_c = away(cols, slot_r), away(cols_c, slot_c)
    per = 2 * SLOT
    chip, chip_c = cols // row_tiles >> 1 == me >> 1, cols_c // row_tiles >> 1 == me >> 1
    near, near_c = valid & chip, valid_c & chip_c
    far, far_c = valid & ~chip, valid_c & ~chip_c
    write_list(
        out_ref, 0, rows, rows_c, near, near_c, row_tiles, cols_c % (2 * row_tiles), 2 * row_tiles
    )
    write_list(
        out_ref, 1, rows, rows_c, far, far_c, row_tiles, away_c - per, (n_chip - 1) * per
    )
    own, own_c = valid & (cols // row_tiles == me), valid_c & (cols_c // row_tiles == me)
    other, other_c = valid & (cols // row_tiles != me), valid_c & (cols_c // row_tiles != me)
    write_list(out_ref, 2, away_r, away_c, other, other_c, n_chip * per, rows_c, row_tiles)
    write_list(
        out_ref, 3, cols % row_tiles, cols_c % row_tiles, own, own_c, row_tiles, rows_c, row_tiles
    )


def sparse_loop(list_ref, which, x_ref, tiles_ref, acc_ref, forward):
    def step(s, carry):
        for u in range(UNROLL):
            p = 2 * (s * UNROLL + u)
            w0 = list_ref[which, p]
            w1 = list_ref[which, p + 1]
            x = jnp.concatenate([x_ref[(w0 >> 10) & 1023], x_ref[(w1 >> 10) & 1023]], axis=1)
            t0, t1 = tiles_ref[w0 & 1023], tiles_ref[w1 & 1023]
            if forward:
                part = lax.dot_general(
                    x,
                    jnp.concatenate([t0, t1], axis=1),
                    (((1,), (1,)), ((), ())),
                    preferred_element_type=F32,
                )
            else:
                part = jnp.dot(x, jnp.concatenate([t0, t1], axis=0), preferred_element_type=F32)
            acc_ref[w0 >> 20] += part
        return carry

    lax.fori_loop(0, list_ref[4 + which, 0], step, 0)


def load_kernel(in_ref, out_ref, sems):
    n = in_ref.shape[0] // LOADS
    copies = [
        pltpu.make_async_copy(
            in_ref.at[pl.ds(i * n, n)], out_ref.at[pl.ds(i * n, n)], sems.at[i]
        )
        for i in range(LOADS)
    ]
    for c in copies:
        c.start()
    for c in copies:
        c.wait()


def pack_kernel(me_ref, feat_ref, sib_ref, out_ref):
    tiles = feat_ref.shape[1] // TILE
    base = (me_ref[0] & 1) * tiles
    for k in range(tiles):
        out_ref[base + k] = feat_ref[:, k * TILE : (k + 1) * TILE]
        out_ref[tiles - base + k] = sib_ref[:, k * TILE : (k + 1) * TILE]
    out_ref[2 * tiles] = jnp.zeros_like(out_ref[0])


def send_kernel(n_chip, row_tiles, me_ref, *refs):
    need_refs, x_ref, outs = refs[: n_chip - 1], refs[n_chip - 1], refs[n_chip:]
    for need_ref, out in zip(need_refs, outs):
        for q in range(2):
            for j in range(SLOT):
                out[q * SLOT + j] = x_ref[
                    q * row_tiles + need_ref[((me_ref[0] >> 1) << 1) + q, j]
                ]


def fill_from_wide(x_ref, wide_ref, count):
    for k in range(count):
        x_ref[k] = wide_ref[:, k * TILE : (k + 1) * TILE]
    x_ref[count] = jnp.zeros_like(x_ref[count])


def near_fwd_kernel(list_ref, tiles_ref, x_ref, acc_ref):
    acc_ref[...] = jnp.zeros_like(acc_ref)
    sparse_loop(list_ref, 0, x_ref, tiles_ref, acc_ref, True)


def own_bwd_kernel(list_ref, tiles_ref, wide_ref, acc_ref, x_ref):
    fill_from_wide(x_ref, wide_ref, x_ref.shape[0] - 1)
    acc_ref[...] = jnp.zeros_like(acc_ref)
    sparse_loop(list_ref, 3, x_ref, tiles_ref, acc_ref, False)


def far_fwd_kernel(n_in, list_ref, me_ref, tiles_ref, *refs):
    ins, base_ref, rest = refs[:n_in], refs[n_in], refs[n_in + 1 :]
    outs, (x_ref, acc_ref) = rest[:-2], rest[-2:]
    per = 2 * SLOT
    for d, r in enumerate(ins):
        x_ref[d * per : (d + 1) * per] = r[...]
    x_ref[n_in * per] = jnp.zeros_like(x_ref[0])
    acc_ref[...] = base_ref[...]
    sparse_loop(list_ref, 1, x_ref, tiles_ref, acc_ref, True)
    per = acc_ref.shape[0] // len(outs)
    for k, out in enumerate(outs):
        block = me_ref[0] ^ k
        for i in range(per):
            out[:, i * TILE : (i + 1) * TILE] = acc_ref[block * per + i].astype(BF)


def weight_kernel(me_ref, s_ref, z_ref, own_ref, sib_ref):
    n_chip, per, _ = own_ref.shape
    z = z_ref[...]
    for q, out in enumerate((own_ref, sib_ref)):
        core = (me_ref[0] & 1) ^ q
        for c in range(n_chip):
            rows = pl.ds(pl.multiple_of((2 * c + core) * per, per), per)
            out[c] = lax.dot_general(
                s_ref[rows, :], z, (((1,), (1,)), ((), ())), preferred_element_type=F32
            ).astype(out.dtype)


def weight_pair_kernel(me_ref, own_ref, got_ref, keep_ref, *outs):
    for e in range(len(outs) + 1):
        c = (me_ref[0] >> 1) ^ e
        total = own_ref[c] + got_ref[c].astype(F32)
        if e == 0:
            keep_ref[...] = total
        else:
            outs[e - 1][...] = total.astype(BF)


def far_bwd_kernel(n_col, list_ref, mec_ref, mer_ref, tiles_ref, *refs):
    ins, rest = refs[:n_col], refs[n_col:]
    wide_ref, sib_ref, (x_ref, acc_ref) = rest[0], rest[1], rest[-2:]
    outs = rest[2:-2]
    per = 2 * SLOT
    gather_blocks(wide_ref, mec_ref[0], ins)
    fill_from_wide(x_ref, wide_ref, x_ref.shape[0] - 1)
    acc_ref[...] = jnp.zeros_like(acc_ref)
    sparse_loop(list_ref, 2, x_ref, tiles_ref, acc_ref, False)
    for e, out in enumerate(outs):
        out[...] = acc_ref[(e + 1) * per : (e + 2) * per].astype(BF)
    other = 1 - (mer_ref[0] & 1)
    for j in range(SLOT):
        sib_ref[j] = acc_ref[other * SLOT + j].astype(BF)


def forward_kernel(me_ref, *refs):
    other = 1 - (me_ref[0] & 1)
    for e, r in enumerate(refs[:-1]):
        for j in range(SLOT):
            refs[-1][e * SLOT + j] = r[other * SLOT + j]


def join_kernel(n_chip, me_ref, table_ref, base_ref, sib_ref, fwd_ref, *refs):
    ins, (out_ref, acc_ref) = refs[:-2], refs[-2:]
    me = me_ref[0]
    core = me & 1
    n_row = 2 * n_chip

    def tile(e, j, other):
        return table_ref[(other * n_chip + e) * n_row + me, j]

    acc_ref[...] = base_ref[...]
    for j in range(SLOT):
        acc_ref[tile(0, j, 1)] += sib_ref[j].astype(F32)
        for e, r in enumerate(ins):
            acc_ref[tile(e + 1, j, 0)] += r[core * SLOT + j].astype(F32)
            acc_ref[tile(e + 1, j, 1)] += fwd_ref[e * SLOT + j].astype(F32)
    for k in range(acc_ref.shape[0]):
        out_ref[:, k * TILE : (k + 1) * TILE] = acc_ref[k].astype(BF)


def pair_kernel(me_ref, own_ref, sib_ref, out_ref):
    core = me_ref[0] & 1
    out_ref[core] = own_ref[...]
    out_ref[1 - core] = sib_ref[...]


def weight_place_kernel(me_ref, *refs):
    out_ref = refs[-1]
    per = refs[0].shape[1]
    for e, r in enumerate(refs[:-1]):
        for q in range(2):
            row = (((me_ref[0] >> 1) ^ e) << 1) + q
            out_ref[pl.ds(pl.multiple_of(row * per, per), per), :] = r[q]


def dense_kernel(n_col, me_ref, wt_ref, w_ref, *refs):
    s_refs, g_refs = refs[:n_col], refs[n_col : 2 * n_col]
    o_refs, y_refs = refs[2 * n_col : 3 * n_col], refs[3 * n_col : 4 * n_col]
    z_ref, s_ref = refs[4 * n_col], refs[4 * n_col + 1]
    f_loc = s_refs[0].shape[0]
    me = me_ref[0]
    for k in range(n_col):
        s_ref[pl.ds(pl.multiple_of((me ^ k) * f_loc, f_loc), f_loc), :] = s_refs[k][...]
    s_all = s_ref[...]
    for k in range(n_col):
        rows = pl.ds(pl.multiple_of((me ^ k) * f_loc, f_loc), f_loc)
        pre = jnp.dot(wt_ref[rows, :], s_all, preferred_element_type=F32)
        sig = 1.0 / (1.0 + jnp.exp(-pre))
        o_refs[k][...] = (pre * sig).astype(BF)
        slope = sig * (1.0 + pre * (1.0 - sig))
        z_ref[rows, :] = (g_refs[k][...].astype(F32) * slope).astype(BF)
    z_all = z_ref[...]
    for k in range(n_col):
        rows = pl.ds(pl.multiple_of((me ^ k) * f_loc, f_loc), f_loc)
        y_refs[k][...] = jnp.dot(w_ref[rows, :], z_all, preferred_element_type=F32).astype(BF)


def gather_blocks(wide_ref, me, refs):
    width = refs[0].shape[1]
    for k, r in enumerate(refs):
        wide_ref[:, pl.ds(pl.multiple_of((me ^ k) * width, width), width)] = r[...]


def place_kernel(me_ref, *refs):
    wide_ref = refs[-1]
    width = refs[0].shape[1]
    for k, r in enumerate(refs[:-1]):
        at = pl.multiple_of((me_ref[0] ^ k) * width, width)
        wide_ref[:, pl.ds(at, width)] = r[: wide_ref.shape[0], :]


def split_kernel(me_ref, x_ref, *outs):
    width = outs[0].shape[1]
    for k, out in enumerate(outs):
        out[...] = x_ref[:, pl.ds(pl.multiple_of((me_ref[0] ^ k) * width, width), width)]


def weight_cols_kernel(n_chip, me_ref, *refs):
    n_col = (len(refs) - n_chip - 2) // 2
    ins, o_refs = refs[:n_chip], refs[n_chip : n_chip + n_col]
    outs, own_ref, sum_ref = refs[n_chip + n_col : -2], refs[-2], refs[-1]
    total = ins[0][...]
    for r in ins[1:]:
        total += r[...].astype(F32)
    sum_ref[...] = total
    h_loc, part = o_refs[0].shape
    rows = total.shape[0] * h_loc // part
    for k, out in enumerate(outs):
        if k:
            out[:h_loc, :] = o_refs[k][...]
        for c in range(n_col):

            @pl.when(me_ref[0] ^ k == c)
            def _():
                mine = sum_ref[:, c * h_loc : (c + 1) * h_loc]
                if k == 0:
                    own_ref[...] = mine
                else:
                    for i in range(part // h_loc):
                        out[h_loc : h_loc + rows, i * h_loc : (i + 1) * h_loc] = mine[
                            i * rows : (i + 1) * rows
                        ].astype(BF)


def weight_scale_kernel(scale, own_ref, *refs):
    out_ref = refs[-1]
    n_rows, h_loc = own_ref.shape
    rows = n_rows * h_loc // refs[0].shape[1]
    for i in range(n_rows // rows):
        total = own_ref[i * rows : (i + 1) * rows, :]
        for r in refs[:-1]:
            total += r[h_loc : h_loc + rows, i * h_loc : (i + 1) * h_loc].astype(F32)
        out_ref[i * rows : (i + 1) * rows, :] = total * scale


def shards(features, weight, tile_cols, tile_rows, tile_count, tile_values, out_grad):
    n_row, n_col = lax.axis_size("row"), lax.axis_size("col")
    n_chip = n_row // 2
    me_r, me_c = lax.axis_index("row").astype(jnp.int32), lax.axis_index("col").astype(jnp.int32)
    mer, mec = me_r.reshape(1), me_c.reshape(1)
    f_loc, nodes = features.shape
    h_loc = out_grad.shape[0]
    n_f, n_h = weight.shape
    row_tiles = nodes // TILE
    part = nodes // n_col
    slots = tile_cols.shape[1]
    per = 2 * SLOT
    sds = jax.ShapeDtypeStruct
    tile_flops = 2 * f_loc * TILE * TILE
    tile_bytes = slots * TILE * TILE * 2

    tile_values, mer, mec, weight_t = lax.optimization_barrier(
        (tile_values, mer, mec, weight.T)
    )
    tile_values = pl.pallas_call(
        load_kernel,
        out_shape=sds(tile_values.shape, BF),
        in_specs=[pl.BlockSpec(memory_space=pltpu.HBM)],
        out_specs=VM,
        scratch_shapes=[pltpu.SemaphoreType.DMA((LOADS,))],
        compiler_params=pltpu.CompilerParams(vmem_limit_bytes=24 << 20),
        cost_estimate=pl.CostEstimate(flops=0, bytes_accessed=tile_bytes, transcendentals=0),
    )(pltpu.with_memory_space_constraint(tile_values, pltpu.HBM))

    def over_chips(x):
        return swap(x, "row", n_row, 1)

    sib_feat = over_chips(features)
    need = call(
        functools.partial(need_kernel, n_row, row_tiles),
        sds((n_row, 128), jnp.int32),
        [],
        (tile_count,),
        (tile_cols,),
    )
    needs = [need] + [swap(need, "row", n_row, 2 * e) for e in range(1, n_chip)]
    length = -(-(slots + n_chip * per + 2 * UNROLL) // 128) * 128
    lists = call(
        functools.partial(lists_kernel, n_row, row_tiles),
        sds((8, length), jnp.int32),
        [],
        (tile_count, mer),
        (tile_cols, tile_rows),
    )
    x_near = call(
        pack_kernel,
        sds((2 * row_tiles + 1, f_loc, TILE), BF),
        [],
        (mer,),
        (features, sib_feat),
        nbytes=f_loc * nodes * 8,
    )
    g_parts = call(
        split_kernel,
        [sds((h_loc, part), BF)] * n_col,
        [],
        (mec,),
        (out_grad,),
        nbytes=h_loc * nodes * 4,
    )
    needs, x_near, lists, tile_values, g_parts = lax.optimization_barrier(
        (needs, x_near, lists, tile_values, g_parts)
    )
    sends = call(
        functools.partial(send_kernel, n_chip, row_tiles),
        [sds((per, f_loc, TILE), BF)] * (n_chip - 1),
        [],
        (mer, *needs[1:]),
        (x_near,),
        nbytes=4 * n_chip * per * f_loc * TILE,
    )
    got = [swap(x, "row", n_row, 2 * (e + 1)) for e, x in enumerate(sends)]
    table = jnp.concatenate(needs, axis=0)
    table = jnp.concatenate([table, over_chips(table)], axis=0)
    got, table = lax.optimization_barrier((got, table))

    grads = [g if k == 0 else swap(g, "col", n_col, k) for k, g in enumerate(g_parts)]

    acc = call(
        near_fwd_kernel,
        sds((row_tiles, f_loc, TILE), F32),
        [],
        (lists,),
        (x_near,),
        (tile_values,),
        flops=tile_flops * slots,
        nbytes=tile_bytes,
    )
    s_parts = call(
        functools.partial(far_fwd_kernel, n_chip - 1),
        [sds((f_loc, part), BF)] * n_col,
        [
            pltpu.VMEM(((n_chip - 1) * per + 1, f_loc, TILE), BF),
            pltpu.VMEM((row_tiles, f_loc, TILE), F32),
        ],
        (lists, mec),
        (*got, acc),
        (tile_values,),
        flops=tile_flops * slots,
        nbytes=tile_bytes,
    )
    s_got = [s if k == 0 else swap(s, "col", n_col, k) for k, s in enumerate(s_parts)]

    res = call(
        functools.partial(dense_kernel, n_col),
        [sds((h_loc, part), BF)] * n_col
        + [sds((f_loc, part), BF)] * n_col
        + [sds((n_h, part), BF), sds((n_f, part), BF)],
        [],
        (mec,),
        (weight_t, weight, *s_got, *grads),
        flops=4 * n_f * n_h * part,
        nbytes=n_f * part * 8,
    )
    o_parts, y_parts, z_all, s_all = res[:n_col], res[n_col : 2 * n_col], res[-2], res[-1]
    y_got = [y if k == 0 else swap(y, "col", n_col, k) for k, y in enumerate(y_parts)]

    w_rows = n_f // n_row
    w_own, w_sib = call(
        weight_kernel,
        [sds((n_chip, w_rows, n_h), F32), sds((n_chip, w_rows, n_h), BF)],
        [],
        (mer,),
        (s_all, z_all),
        flops=2 * n_f * n_h * part,
        nbytes=n_f * part * 8,
    )
    w_parts = call(
        weight_pair_kernel,
        [sds((w_rows, n_h), F32)] + [sds((w_rows, n_h), BF)] * (n_chip - 1),
        [],
        (mer,),
        (w_own, over_chips(w_sib)),
        nbytes=n_f * n_h * 4,
    )
    w_chips = [w if e == 0 else swap(w, "row", n_row, 2 * e) for e, w in enumerate(w_parts)]
    more = -(-(w_rows * h_loc // part) // 16) * 16
    mixed = call(
        functools.partial(weight_cols_kernel, n_chip),
        [sds((h_loc + more, part), BF)] * n_col + [sds((w_rows, h_loc), F32)],
        [pltpu.VMEM((w_rows, n_h), F32)],
        (mec,),
        (*w_chips, *o_parts),
        nbytes=n_h * part * 4,
    )
    w_own_cols = mixed[-1]
    mixed = [m if k == 0 else swap(m, "col", n_col, k) for k, m in enumerate(mixed[:-1])]

    y_got, w_chips = lax.optimization_barrier((y_got, w_chips))
    back = call(
        functools.partial(far_bwd_kernel, n_col),
        [sds((f_loc, nodes), BF), sds((SLOT, f_loc, TILE), BF)]
        + [sds((per, f_loc, TILE), BF)] * (n_chip - 1),
        [
            pltpu.VMEM((row_tiles + 1, f_loc, TILE), BF),
            pltpu.VMEM((n_chip * per, f_loc, TILE), F32),
        ],
        (lists, mec, mer),
        tuple(y_got),
        (tile_values,),
        flops=tile_flops * slots,
        nbytes=tile_bytes,
    )
    y_wide, to_sib, contribs = back[0], back[1], back[2:]
    returned = [swap(x, "row", n_row, 2 * (e + 1)) for e, x in enumerate(contribs)]
    from_sib = over_chips(to_sib)

    w_mine = call(
        functools.partial(weight_scale_kernel, float(nodes * n_row) ** (-0.5)),
        sds((w_rows, h_loc), F32),
        [],
        (),
        (w_own_cols, *mixed[1:]),
    )

    w_mine = call(
        functools.partial(weight_scale_kernel, float(nodes * n_row) ** (-0.5)),
        sds((w_rows, h_loc), F32),
        [],
        (),
        (w_own_cols, *mixed[1:]),
    )

    o_parts, _ = lax.optimization_barrier((o_parts, to_sib))
    o_got = [o if k == 0 else swap(o, "col", n_col, k) for k, o in enumerate(o_parts)]
    acc_b = call(
        own_bwd_kernel,
        sds((row_tiles, f_loc, TILE), F32),
        [pltpu.VMEM((row_tiles + 1, f_loc, TILE), BF)],
        (lists,),
        (y_wide,),
        (tile_values,),
        flops=tile_flops * slots,
        nbytes=tile_bytes,
    )
    returned, acc_b, w_mine = lax.optimization_barrier((returned, acc_b, w_mine))
    passed = call(
        forward_kernel,
        sds(((n_chip - 1) * SLOT, f_loc, TILE), BF),
        [],
        (mer,),
        tuple(returned),
    )
    w_pair = call(
        pair_kernel, sds((2, w_rows, h_loc), F32), [], (mer,), (w_mine, over_chips(w_mine))
    )
    w_chips = [w_pair] + [swap(w_pair, "row", n_row, 2 * e) for e in range(1, n_chip)]
    weight_grad = call(
        weight_place_kernel,
        sds((n_f, h_loc), F32),
        [],
        (mer,),
        tuple(w_chips),
        nbytes=n_f * h_loc * 8,
    )

    input_grad = call(
        functools.partial(join_kernel, n_chip),
        sds((f_loc, nodes), BF),
        [pltpu.VMEM((row_tiles, f_loc, TILE), F32)],
        (mer, table),
        (acc_b, from_sib, over_chips(passed), *returned),
        nbytes=f_loc * nodes * 8,
    )
    output = call(
        place_kernel, sds((h_loc, nodes), BF), [], (mec,), (o_parts[0], *mixed[1:]), nbytes=h_loc * nodes * 4
    )
    return output, input_grad, weight_grad


def solution(mesh):
    return jax.shard_map(
        shards,
        mesh=mesh,
        in_specs=(
            P("col", "row"),
            P(),
            P("row", None),
            P("row", None),
            P("row"),
            P("row", None, None),
            P("col", "row"),
        ),
        out_specs=(P("col", "row"), P("col", "row"), P(None, "col")),
        check_vma=False,
    )
```

```python
import functools

import jax
import jax.numpy as jnp
from jax import lax
from jax.experimental import pallas as pl
from jax.experimental.pallas import tpu as pltpu
from jax.sharding import PartitionSpec as P

TILE = 128
SLOT = 4
UNROLL = 4
LOADS = 8
BF = jnp.bfloat16
F32 = jnp.float32
VM = pl.BlockSpec(memory_space=pltpu.VMEM)
SM = pl.BlockSpec(memory_space=pltpu.SMEM)


def call(kernel, outs, scratch, smem, vmem, held=(), flops=0, nbytes=0, limit=24):
    return pl.pallas_call(
        kernel,
        out_shape=outs,
        in_specs=[SM] * len(smem) + [VM] * len(held) + [VM] * len(vmem),
        out_specs=jax.tree.map(lambda _: VM, outs),
        scratch_shapes=scratch,
        compiler_params=pltpu.CompilerParams(vmem_limit_bytes=limit << 20),
        cost_estimate=pl.CostEstimate(flops=flops, bytes_accessed=nbytes, transcendentals=0),
    )(*[pltpu.with_memory_space_constraint(x, pltpu.SMEM) for x in smem], *held, *vmem)


def swap(x, axis, n, k):
    return lax.ppermute(x, axis, [(i, i ^ k) for i in range(n)])


def flip(x, n):
    i = lax.broadcasted_iota(jnp.int32, (n, n), 0)
    j = lax.broadcasted_iota(jnp.int32, (n, n), 1)
    return jnp.sum(jnp.where(i == j, x, 0), axis=1 if x.shape[0] == 1 else 0, keepdims=True)


def iota(n, axis):
    return lax.broadcasted_iota(jnp.int32, (n, 1) if axis == 0 else (1, n), axis)


def ranks(cols, valid, blocks, row_tiles):
    b_col, b_row = iota(blocks, 0), iota(blocks, 1)
    hit = jnp.where((cols == b_col) & valid, 1, 0)
    used_col = jnp.max(hit, axis=1, keepdims=True)
    used_row = flip(used_col, blocks)
    same = (b_col // row_tiles) == (b_row // row_tiles)
    rank_row = jnp.sum(jnp.where(same & (b_col < b_row), used_col, 0), axis=0, keepdims=True)
    rank_col = jnp.sum(jnp.where(same & (b_row < b_col), used_row, 0), axis=1, keepdims=True)
    return used_row, rank_row, rank_col


def need_kernel(n_row, row_tiles, count_ref, cols_ref, need_ref):
    cols = cols_ref[...]
    blocks = n_row * row_tiles
    valid = iota(cols.shape[1], 1) < count_ref[0]
    used, rank, _ = ranks(cols, valid, blocks, row_tiles)
    b = iota(blocks, 1)
    owner = (b // row_tiles) == iota(n_row, 0)
    lane = iota(128, 1)
    total = jnp.zeros((n_row, 128), jnp.int32)
    for j in range(SLOT):
        pick = jnp.where((used > 0) & (rank == j), b % row_tiles, 0)
        total += jnp.where(
            lane == j, jnp.sum(jnp.where(owner, pick, 0), axis=1, keepdims=True), 0
        )
    need_ref[...] = total


def write_list(out_ref, which, key_row, key_col, valid_row, valid_col, groups, source, blank):
    slots, length = key_row.shape[1], out_ref.shape[1]
    t_row, t_col = iota(slots, 1), iota(slots, 0)
    key_row, key_col = jnp.where(valid_row, key_row, -1), jnp.where(valid_col, key_col, -1)
    g_col, g_row = iota(groups, 0), iota(128, 1)
    count = jnp.sum(jnp.where(key_row == g_col, 1, 0), axis=1, keepdims=True)
    even = ((count + 1) >> 1) << 1
    start = jnp.sum(jnp.where(g_col < g_row, even, 0), axis=0, keepdims=True)
    first = jnp.sum(jnp.where(key_col == g_row, start, 0), axis=1, keepdims=True)
    rank = jnp.sum(jnp.where((key_row == key_col) & (t_row < t_col), 1, 0), axis=1, keepdims=True)
    place = jnp.where(valid_col, first + rank, -1)
    word = t_col | (source << 10) | (key_col << 20)
    pad = blank << 10
    words = jnp.sum(jnp.where(place == iota(length, 1), word - pad, 0), axis=0, keepdims=True) + pad
    out_ref[which : which + 1, :] = words
    total = jnp.sum(even, axis=0, keepdims=True)
    steps = (total + (2 * UNROLL - 1)) // (2 * UNROLL)
    out_ref[4 + which : 5 + which, :] = jnp.broadcast_to(steps, (1, length))


def lists_kernel(n_row, row_tiles, count_ref, me_ref, cols_ref, rows_ref, out_ref):
    cols, rows = cols_ref[...], rows_ref[...]
    slots = cols.shape[1]
    blocks = n_row * row_tiles
    me, n_chip = me_ref[0], n_row // 2
    valid = iota(slots, 1) < count_ref[0]
    _, rank_row, rank_col = ranks(cols, valid, blocks, row_tiles)
    cols_c, rows_c = flip(cols, slots), flip(rows, slots)
    valid_c = iota(slots, 0) < count_ref[0]
    slot_c = jnp.sum(jnp.where(cols_c == iota(blocks, 1), rank_row, 0), axis=1, keepdims=True)
    slot_r = jnp.sum(jnp.where(cols == iota(blocks, 0), rank_col, 0), axis=0, keepdims=True)

    def away(c, s):
        owner = c // row_tiles
        return ((owner >> 1) ^ (me >> 1)) * (2 * SLOT) + (owner & 1) * SLOT + s

    away_r, away_c = away(cols, slot_r), away(cols_c, slot_c)
    per = 2 * SLOT
    chip, chip_c = cols // row_tiles >> 1 == me >> 1, cols_c // row_tiles >> 1 == me >> 1
    near, near_c = valid & chip, valid_c & chip_c
    far, far_c = valid & ~chip, valid_c & ~chip_c
    write_list(
        out_ref, 0, rows, rows_c, near, near_c, row_tiles, cols_c % (2 * row_tiles), 2 * row_tiles
    )
    write_list(
        out_ref, 1, rows, rows_c, far, far_c, row_tiles, away_c - per, (n_chip - 1) * per
    )
    own, own_c = valid & (cols // row_tiles == me), valid_c & (cols_c // row_tiles == me)
    other, other_c = valid & (cols // row_tiles != me), valid_c & (cols_c // row_tiles != me)
    write_list(out_ref, 2, away_r, away_c, other, other_c, n_chip * per, rows_c, row_tiles)
    write_list(
        out_ref, 3, cols % row_tiles, cols_c % row_tiles, own, own_c, row_tiles, rows_c, row_tiles
    )


def sparse_loop(list_ref, which, x_ref, tiles_ref, acc_ref, forward):
    def step(s, carry):
        for u in range(UNROLL):
            p = 2 * (s * UNROLL + u)
            w0 = list_ref[which, p]
            w1 = list_ref[which, p + 1]
            x = jnp.concatenate([x_ref[(w0 >> 10) & 1023], x_ref[(w1 >> 10) & 1023]], axis=1)
            t0, t1 = tiles_ref[w0 & 1023], tiles_ref[w1 & 1023]
            if forward:
                part = lax.dot_general(
                    x,
                    jnp.concatenate([t0, t1], axis=1),
                    (((1,), (1,)), ((), ())),
                    preferred_element_type=F32,
                )
            else:
                part = jnp.dot(x, jnp.concatenate([t0, t1], axis=0), preferred_element_type=F32)
            acc_ref[w0 >> 20] += part
        return carry

    lax.fori_loop(0, list_ref[4 + which, 0], step, 0)


def load_kernel(in_ref, out_ref, sems):
    n = in_ref.shape[0] // LOADS
    copies = [
        pltpu.make_async_copy(
            in_ref.at[pl.ds(i * n, n)], out_ref.at[pl.ds(i * n, n)], sems.at[i]
        )
        for i in range(LOADS)
    ]
    for c in copies:
        c.start()
    for c in copies:
        c.wait()


def pack_kernel(me_ref, feat_ref, sib_ref, out_ref):
    tiles = feat_ref.shape[1] // TILE
    base = (me_ref[0] & 1) * tiles
    for k in range(tiles):
        out_ref[base + k] = feat_ref[:, k * TILE : (k + 1) * TILE]
        out_ref[tiles - base + k] = sib_ref[:, k * TILE : (k + 1) * TILE]
    out_ref[2 * tiles] = jnp.zeros_like(out_ref[0])


def send_kernel(n_chip, row_tiles, me_ref, *refs):
    need_refs, x_ref, outs = refs[: n_chip - 1], refs[n_chip - 1], refs[n_chip:]
    for need_ref, out in zip(need_refs, outs):
        for q in range(2):
            for j in range(SLOT):
                out[q * SLOT + j] = x_ref[
                    q * row_tiles + need_ref[((me_ref[0] >> 1) << 1) + q, j]
                ]


def fill_from_wide(x_ref, wide_ref, count):
    for k in range(count):
        x_ref[k] = wide_ref[:, k * TILE : (k + 1) * TILE]
    x_ref[count] = jnp.zeros_like(x_ref[count])


def near_fwd_kernel(list_ref, tiles_ref, x_ref, acc_ref):
    acc_ref[...] = jnp.zeros_like(acc_ref)
    sparse_loop(list_ref, 0, x_ref, tiles_ref, acc_ref, True)


def own_bwd_kernel(list_ref, tiles_ref, wide_ref, acc_ref, x_ref):
    fill_from_wide(x_ref, wide_ref, x_ref.shape[0] - 1)
    acc_ref[...] = jnp.zeros_like(acc_ref)
    sparse_loop(list_ref, 3, x_ref, tiles_ref, acc_ref, False)


def far_fwd_kernel(n_in, list_ref, me_ref, tiles_ref, *refs):
    ins, base_ref, rest = refs[:n_in], refs[n_in], refs[n_in + 1 :]
    outs, (x_ref, acc_ref) = rest[:-2], rest[-2:]
    per = 2 * SLOT
    for d, r in enumerate(ins):
        x_ref[d * per : (d + 1) * per] = r[...]
    x_ref[n_in * per] = jnp.zeros_like(x_ref[0])
    acc_ref[...] = base_ref[...]
    sparse_loop(list_ref, 1, x_ref, tiles_ref, acc_ref, True)
    per = acc_ref.shape[0] // len(outs)
    for k, out in enumerate(outs):
        block = me_ref[0] ^ k
        for i in range(per):
            out[:, i * TILE : (i + 1) * TILE] = acc_ref[block * per + i].astype(BF)


def weight_kernel(me_ref, own_ref, sib_ref, keep_ref, *outs):
    n_f = own_ref.shape[0] - keep_ref.shape[1]
    per = keep_ref.shape[0]
    core = me_ref[0] & 1
    pairs = [(r, r[n_f:, :]) for r in (own_ref, sib_ref)]
    for e in range(len(outs) + 1):
        row = ((((me_ref[0] >> 1) ^ e) << 1) + core) * per
        rows = pl.ds(pl.multiple_of(row, per), per)
        total = sum(
            lax.dot_general(r[rows, :], z, (((1,), (1,)), ((), ())), preferred_element_type=F32)
            for r, z in pairs
        )
        if e == 0:
            keep_ref[...] = total
        else:
            outs[e - 1][...] = total.astype(BF)


def far_bwd_kernel(n_col, list_ref, mec_ref, mer_ref, tiles_ref, *refs):
    ins, rest = refs[:n_col], refs[n_col:]
    wide_ref, sib_ref, (x_ref, acc_ref) = rest[0], rest[1], rest[-2:]
    outs = rest[2:-2]
    per = 2 * SLOT
    gather_blocks(wide_ref, mec_ref[0], ins)
    fill_from_wide(x_ref, wide_ref, x_ref.shape[0] - 1)
    acc_ref[...] = jnp.zeros_like(acc_ref)
    sparse_loop(list_ref, 2, x_ref, tiles_ref, acc_ref, False)
    for e, out in enumerate(outs):
        out[...] = acc_ref[(e + 1) * per : (e + 2) * per].astype(BF)
    other = 1 - (mer_ref[0] & 1)
    for j in range(SLOT):
        sib_ref[j] = acc_ref[other * SLOT + j].astype(BF)


def forward_kernel(me_ref, *refs):
    other = 1 - (me_ref[0] & 1)
    for e, r in enumerate(refs[:-1]):
        for j in range(SLOT):
            refs[-1][e * SLOT + j] = r[other * SLOT + j]


def join_kernel(n_chip, me_ref, table_ref, base_ref, sib_ref, fwd_ref, *refs):
    ins, (out_ref, acc_ref) = refs[:-2], refs[-2:]
    me = me_ref[0]
    core = me & 1
    n_row = 2 * n_chip

    def tile(e, j, other):
        return table_ref[(other * n_chip + e) * n_row + me, j]

    acc_ref[...] = base_ref[...]
    for j in range(SLOT):
        acc_ref[tile(0, j, 1)] += sib_ref[j].astype(F32)
        for e, r in enumerate(ins):
            acc_ref[tile(e + 1, j, 0)] += r[core * SLOT + j].astype(F32)
            acc_ref[tile(e + 1, j, 1)] += fwd_ref[e * SLOT + j].astype(F32)
    for k in range(acc_ref.shape[0]):
        out_ref[:, k * TILE : (k + 1) * TILE] = acc_ref[k].astype(BF)


def pair_kernel(me_ref, own_ref, sib_ref, out_ref):
    core = me_ref[0] & 1
    out_ref[core] = own_ref[...]
    out_ref[1 - core] = sib_ref[...]


def weight_place_kernel(me_ref, *refs):
    out_ref = refs[-1]
    per = refs[0].shape[1]
    for e, r in enumerate(refs[:-1]):
        for q in range(2):
            row = (((me_ref[0] >> 1) ^ e) << 1) + q
            out_ref[pl.ds(pl.multiple_of(row * per, per), per), :] = r[q]


def dense_kernel(n_col, me_ref, wt_ref, w_ref, *refs):
    s_refs, g_refs = refs[:n_col], refs[n_col : 2 * n_col]
    o_refs, y_refs = refs[2 * n_col : 3 * n_col], refs[3 * n_col : 4 * n_col]
    sz_ref = refs[4 * n_col]
    f_loc = s_refs[0].shape[0]
    n_f = f_loc * n_col
    s_ref, z_ref = sz_ref.at[pl.ds(0, n_f)], sz_ref.at[pl.ds(n_f, sz_ref.shape[0] - n_f)]
    me = me_ref[0]
    for k in range(n_col):
        s_ref[pl.ds(pl.multiple_of((me ^ k) * f_loc, f_loc), f_loc), :] = s_refs[k][...]
    s_all = s_ref[...]
    for k in range(n_col):
        rows = pl.ds(pl.multiple_of((me ^ k) * f_loc, f_loc), f_loc)
        pre = jnp.dot(wt_ref[rows, :], s_all, preferred_element_type=F32)
        sig = 1.0 / (1.0 + jnp.exp(-pre))
        o_refs[k][...] = (pre * sig).astype(BF)
        slope = sig * (1.0 + pre * (1.0 - sig))
        z_ref[rows, :] = (g_refs[k][...].astype(F32) * slope).astype(BF)
    z_all = z_ref[...]
    for k in range(n_col):
        rows = pl.ds(pl.multiple_of((me ^ k) * f_loc, f_loc), f_loc)
        y_refs[k][...] = jnp.dot(w_ref[rows, :], z_all, preferred_element_type=F32).astype(BF)


def gather_blocks(wide_ref, me, refs):
    width = refs[0].shape[1]
    for k, r in enumerate(refs):
        wide_ref[:, pl.ds(pl.multiple_of((me ^ k) * width, width), width)] = r[...]


def place_kernel(me_ref, *refs):
    wide_ref = refs[-1]
    width = refs[0].shape[1]
    for k, r in enumerate(refs[:-1]):
        at = pl.multiple_of((me_ref[0] ^ k) * width, width)
        wide_ref[:, pl.ds(at, width)] = r[: wide_ref.shape[0], :]


def turn_kernel(x_ref, out_ref):
    out_ref[...] = x_ref[...].T


def split_kernel(me_ref, x_ref, *outs):
    width = outs[0].shape[1]
    for k, out in enumerate(outs):
        out[...] = x_ref[:, pl.ds(pl.multiple_of((me_ref[0] ^ k) * width, width), width)]


def weight_cols_kernel(n_chip, me_ref, *refs):
    n_col = (len(refs) - n_chip - 2) // 2
    ins, o_refs = refs[:n_chip], refs[n_chip : n_chip + n_col]
    outs, own_ref, sum_ref = refs[n_chip + n_col : -2], refs[-2], refs[-1]
    total = ins[0][...]
    for r in ins[1:]:
        total += r[...].astype(F32)
    sum_ref[...] = total
    h_loc, part = o_refs[0].shape
    rows = total.shape[0] * h_loc // part
    for k, out in enumerate(outs):
        if k:
            out[:h_loc, :] = o_refs[k][...]
        for c in range(n_col):

            @pl.when(me_ref[0] ^ k == c)
            def _():
                mine = sum_ref[:, c * h_loc : (c + 1) * h_loc]
                if k == 0:
                    own_ref[...] = mine
                else:
                    for i in range(part // h_loc):
                        out[h_loc : h_loc + rows, i * h_loc : (i + 1) * h_loc] = mine[
                            i * rows : (i + 1) * rows
                        ].astype(BF)


def weight_scale_kernel(scale, own_ref, *refs):
    out_ref = refs[-1]
    n_rows, h_loc = own_ref.shape
    rows = n_rows * h_loc // refs[0].shape[1]
    for i in range(n_rows // rows):
        total = own_ref[i * rows : (i + 1) * rows, :]
        for r in refs[:-1]:
            total += r[h_loc : h_loc + rows, i * h_loc : (i + 1) * h_loc].astype(F32)
        out_ref[i * rows : (i + 1) * rows, :] = total * scale


def shards(features, weight, tile_cols, tile_rows, tile_count, tile_values, out_grad):
    n_row, n_col = lax.axis_size("row"), lax.axis_size("col")
    n_chip = n_row // 2
    me_r, me_c = lax.axis_index("row").astype(jnp.int32), lax.axis_index("col").astype(jnp.int32)
    mer, mec = me_r.reshape(1), me_c.reshape(1)
    f_loc, nodes = features.shape
    h_loc = out_grad.shape[0]
    n_f, n_h = weight.shape
    row_tiles = nodes // TILE
    part = nodes // n_col
    slots = tile_cols.shape[1]
    per = 2 * SLOT
    sds = jax.ShapeDtypeStruct
    tile_flops = 2 * f_loc * TILE * TILE
    tile_bytes = slots * TILE * TILE * 2

    def over_chips(x):
        return swap(x, "row", n_row, 1)

    sib_feat = over_chips(features)
    need = call(
        functools.partial(need_kernel, n_row, row_tiles),
        sds((n_row, 128), jnp.int32),
        [],
        (tile_count,),
        (tile_cols,),
    )
    mer, mec, need = lax.optimization_barrier((mer, mec, need))
    needs = [need] + [swap(need, "row", n_row, 2 * e) for e in range(1, n_chip)]
    length = -(-(slots + n_chip * per + 2 * UNROLL) // 128) * 128
    x_near = call(
        pack_kernel,
        sds((2 * row_tiles + 1, f_loc, TILE), BF),
        [],
        (mer,),
        (features, sib_feat),
        nbytes=f_loc * nodes * 8,
    )
    tile_values, mer, mec = lax.optimization_barrier((tile_values, mer, mec))
    tile_values = pl.pallas_call(
        load_kernel,
        out_shape=sds(tile_values.shape, BF),
        in_specs=[pl.BlockSpec(memory_space=pltpu.HBM)],
        out_specs=VM,
        scratch_shapes=[pltpu.SemaphoreType.DMA((LOADS,))],
        compiler_params=pltpu.CompilerParams(vmem_limit_bytes=24 << 20),
        cost_estimate=pl.CostEstimate(flops=0, bytes_accessed=tile_bytes, transcendentals=0),
    )(pltpu.with_memory_space_constraint(tile_values, pltpu.HBM))
    needs, x_near, tile_values = lax.optimization_barrier((needs, x_near, tile_values))
    sends = call(
        functools.partial(send_kernel, n_chip, row_tiles),
        [sds((per, f_loc, TILE), BF)] * (n_chip - 1),
        [],
        (mer, *needs[1:]),
        (x_near,),
        nbytes=4 * n_chip * per * f_loc * TILE,
    )
    got = [swap(x, "row", n_row, 2 * (e + 1)) for e, x in enumerate(sends)]
    needs, sends, lists_in, out_grad = lax.optimization_barrier(
        (needs, sends, (tile_cols, tile_rows), out_grad)
    )
    lists = call(
        functools.partial(lists_kernel, n_row, row_tiles),
        sds((8, length), jnp.int32),
        [],
        (tile_count, mer),
        lists_in,
    )
    table = jnp.concatenate(needs, axis=0)
    table = jnp.concatenate([table, over_chips(table)], axis=0)
    got, table = lax.optimization_barrier((got, table))

    g_parts = call(
        split_kernel,
        [sds((h_loc, part), BF)] * n_col,
        [],
        (mec,),
        (out_grad,),
        nbytes=h_loc * nodes * 4,
    )
    grads = [g if k == 0 else swap(g, "col", n_col, k) for k, g in enumerate(g_parts)]

    acc = call(
        near_fwd_kernel,
        sds((row_tiles, f_loc, TILE), F32),
        [],
        (lists,),
        (x_near,),
        (tile_values,),
        flops=tile_flops * slots,
        nbytes=tile_bytes,
    )
    s_parts = call(
        functools.partial(far_fwd_kernel, n_chip - 1),
        [sds((f_loc, part), BF)] * n_col,
        [
            pltpu.VMEM(((n_chip - 1) * per + 1, f_loc, TILE), BF),
            pltpu.VMEM((row_tiles, f_loc, TILE), F32),
        ],
        (lists, mec),
        (*got, acc),
        (tile_values,),
        flops=tile_flops * slots,
        nbytes=tile_bytes,
    )
    s_got = [s if k == 0 else swap(s, "col", n_col, k) for k, s in enumerate(s_parts)]

    weight_t, _ = lax.optimization_barrier((weight, s_parts[0]))
    weight_t = call(turn_kernel, sds((n_h, n_f), BF), [], (), (weight_t,), nbytes=n_f * n_h * 4)
    res = call(
        functools.partial(dense_kernel, n_col),
        [sds((h_loc, part), BF)] * n_col
        + [sds((f_loc, part), BF)] * n_col
        + [sds((n_f + n_h, part), BF)],
        [],
        (mec,),
        (weight_t, weight, *s_got, *grads),
        flops=4 * n_f * n_h * part,
        nbytes=n_f * part * 8,
    )
    o_parts, y_parts, sz = res[:n_col], res[n_col : 2 * n_col], res[-1]
    y_got = [y if k == 0 else swap(y, "col", n_col, k) for k, y in enumerate(y_parts)]

    w_rows = n_f // n_row
    w_parts = call(
        weight_kernel,
        [sds((w_rows, n_h), F32)] + [sds((w_rows, n_h), BF)] * (n_chip - 1),
        [],
        (mer,),
        (sz, over_chips(sz)),
        flops=2 * n_f * n_h * part,
        nbytes=n_f * part * 8,
    )
    w_chips = [w if e == 0 else swap(w, "row", n_row, 2 * e) for e, w in enumerate(w_parts)]
    more = -(-(w_rows * h_loc // part) // 16) * 16
    mixed = call(
        functools.partial(weight_cols_kernel, n_chip),
        [sds((h_loc + more, part), BF)] * n_col + [sds((w_rows, h_loc), F32)],
        [pltpu.VMEM((w_rows, n_h), F32)],
        (mec,),
        (*w_chips, *o_parts),
        nbytes=n_h * part * 4,
    )
    w_own_cols = mixed[-1]
    mixed = [m if k == 0 else swap(m, "col", n_col, k) for k, m in enumerate(mixed[:-1])]

    y_got, w_chips = lax.optimization_barrier((y_got, w_chips))
    back = call(
        functools.partial(far_bwd_kernel, n_col),
        [sds((f_loc, nodes), BF), sds((SLOT, f_loc, TILE), BF)]
        + [sds((per, f_loc, TILE), BF)] * (n_chip - 1),
        [
            pltpu.VMEM((row_tiles + 1, f_loc, TILE), BF),
            pltpu.VMEM((n_chip * per, f_loc, TILE), F32),
        ],
        (lists, mec, mer),
        tuple(y_got),
        (tile_values,),
        flops=tile_flops * slots,
        nbytes=tile_bytes,
    )
    y_wide, to_sib, contribs = back[0], back[1], back[2:]
    returned = [swap(x, "row", n_row, 2 * (e + 1)) for e, x in enumerate(contribs)]
    from_sib = over_chips(to_sib)

    w_mine = call(
        functools.partial(weight_scale_kernel, float(nodes * n_row) ** (-0.5)),
        sds((w_rows, h_loc), F32),
        [],
        (),
        (w_own_cols, *mixed[1:]),
    )

    w_mine = call(
        functools.partial(weight_scale_kernel, float(nodes * n_row) ** (-0.5)),
        sds((w_rows, h_loc), F32),
        [],
        (),
        (w_own_cols, *mixed[1:]),
    )

    o_parts, _ = lax.optimization_barrier((o_parts, to_sib))
    o_got = [o if k == 0 else swap(o, "col", n_col, k) for k, o in enumerate(o_parts)]
    acc_b = call(
        own_bwd_kernel,
        sds((row_tiles, f_loc, TILE), F32),
        [pltpu.VMEM((row_tiles + 1, f_loc, TILE), BF)],
        (lists,),
        (y_wide,),
        (tile_values,),
        flops=tile_flops * slots,
        nbytes=tile_bytes,
    )
    returned, acc_b, w_mine = lax.optimization_barrier((returned, acc_b, w_mine))
    passed = call(
        forward_kernel,
        sds(((n_chip - 1) * SLOT, f_loc, TILE), BF),
        [],
        (mer,),
        tuple(returned),
    )
    w_pair = call(
        pair_kernel, sds((2, w_rows, h_loc), F32), [], (mer,), (w_mine, over_chips(w_mine))
    )
    w_chips = [w_pair] + [swap(w_pair, "row", n_row, 2 * e) for e in range(1, n_chip)]

    input_grad = call(
        functools.partial(join_kernel, n_chip),
        sds((f_loc, nodes), BF),
        [pltpu.VMEM((row_tiles, f_loc, TILE), F32)],
        (mer, table),
        (acc_b, from_sib, over_chips(passed), *returned),
        nbytes=f_loc * nodes * 8,
    )
    w_chips, input_grad = lax.optimization_barrier((w_chips, input_grad))
    weight_grad = call(
        weight_place_kernel,
        sds((n_f, h_loc), F32),
        [],
        (mer,),
        tuple(w_chips),
        nbytes=n_f * h_loc * 8,
    )
    output = call(
        place_kernel, sds((h_loc, nodes), BF), [], (mec,), (o_parts[0], *mixed[1:]), nbytes=h_loc * nodes * 4
    )
    return output, input_grad, weight_grad


def solution(mesh):
    return jax.shard_map(
        shards,
        mesh=mesh,
        in_specs=(
            P("col", "row"),
            P(),
            P("row", None),
            P("row", None),
            P("row"),
            P("row", None, None),
            P("col", "row"),
        ),
        out_specs=(P("col", "row"), P("col", "row"), P(None, "col")),
        check_vma=False,
    )
```

```python
import functools

import jax
import jax.numpy as jnp
from jax import lax
from jax.experimental import pallas as pl
from jax.experimental.pallas import tpu as pltpu
from jax.sharding import PartitionSpec as P

TILE = 128
SLOT = 4
UNROLL = 4
LOADS = 8
BF = jnp.bfloat16
F32 = jnp.float32
VM = pl.BlockSpec(memory_space=pltpu.VMEM)
SM = pl.BlockSpec(memory_space=pltpu.SMEM)


def call(kernel, outs, scratch, smem, vmem, held=(), flops=0, nbytes=0, limit=24):
    return pl.pallas_call(
        kernel,
        out_shape=outs,
        in_specs=[SM] * len(smem) + [VM] * len(held) + [VM] * len(vmem),
        out_specs=jax.tree.map(lambda _: VM, outs),
        scratch_shapes=scratch,
        compiler_params=pltpu.CompilerParams(vmem_limit_bytes=limit << 20),
        cost_estimate=pl.CostEstimate(flops=flops, bytes_accessed=nbytes, transcendentals=0),
    )(*[pltpu.with_memory_space_constraint(x, pltpu.SMEM) for x in smem], *held, *vmem)


def swap(x, axis, n, k):
    return lax.ppermute(x, axis, [(i, i ^ k) for i in range(n)])


def flip(x, n):
    i = lax.broadcasted_iota(jnp.int32, (n, n), 0)
    j = lax.broadcasted_iota(jnp.int32, (n, n), 1)
    return jnp.sum(jnp.where(i == j, x, 0), axis=1 if x.shape[0] == 1 else 0, keepdims=True)


def iota(n, axis):
    return lax.broadcasted_iota(jnp.int32, (n, 1) if axis == 0 else (1, n), axis)


def ranks(cols, valid, blocks, row_tiles):
    b_col, b_row = iota(blocks, 0), iota(blocks, 1)
    hit = jnp.where((cols == b_col) & valid, 1, 0)
    used_col = jnp.max(hit, axis=1, keepdims=True)
    used_row = flip(used_col, blocks)
    same = (b_col // row_tiles) == (b_row // row_tiles)
    rank_row = jnp.sum(jnp.where(same & (b_col < b_row), used_col, 0), axis=0, keepdims=True)
    rank_col = jnp.sum(jnp.where(same & (b_row < b_col), used_row, 0), axis=1, keepdims=True)
    return used_row, rank_row, rank_col


def need_kernel(n_row, row_tiles, count_ref, cols_ref, need_ref):
    cols = cols_ref[...]
    blocks = n_row * row_tiles
    valid = iota(cols.shape[1], 1) < count_ref[0]
    used, rank, _ = ranks(cols, valid, blocks, row_tiles)
    b = iota(blocks, 1)
    owner = (b // row_tiles) == iota(n_row, 0)
    lane = iota(128, 1)
    total = jnp.zeros((n_row, 128), jnp.int32)
    for j in range(SLOT):
        pick = jnp.where((used > 0) & (rank == j), b % row_tiles, 0)
        total += jnp.where(
            lane == j, jnp.sum(jnp.where(owner, pick, 0), axis=1, keepdims=True), 0
        )
    need_ref[...] = total


def write_list(out_ref, which, key_row, key_col, valid_row, valid_col, groups, source, blank):
    slots, length = key_row.shape[1], out_ref.shape[1]
    t_row, t_col = iota(slots, 1), iota(slots, 0)
    key_row, key_col = jnp.where(valid_row, key_row, -1), jnp.where(valid_col, key_col, -1)
    g_col, g_row = iota(groups, 0), iota(128, 1)
    count = jnp.sum(jnp.where(key_row == g_col, 1, 0), axis=1, keepdims=True)
    even = ((count + 1) >> 1) << 1
    start = jnp.sum(jnp.where(g_col < g_row, even, 0), axis=0, keepdims=True)
    first = jnp.sum(jnp.where(key_col == g_row, start, 0), axis=1, keepdims=True)
    rank = jnp.sum(jnp.where((key_row == key_col) & (t_row < t_col), 1, 0), axis=1, keepdims=True)
    place = jnp.where(valid_col, first + rank, -1)
    word = t_col | (source << 10) | (key_col << 20)
    pad = blank << 10
    words = jnp.sum(jnp.where(place == iota(length, 1), word - pad, 0), axis=0, keepdims=True) + pad
    out_ref[which : which + 1, :] = words
    total = jnp.sum(even, axis=0, keepdims=True)
    steps = (total + (2 * UNROLL - 1)) // (2 * UNROLL)
    out_ref[4 + which : 5 + which, :] = jnp.broadcast_to(steps, (1, length))


def lists_kernel(n_row, row_tiles, count_ref, me_ref, cols_ref, rows_ref, out_ref):
    cols, rows = cols_ref[...], rows_ref[...]
    slots = cols.shape[1]
    blocks = n_row * row_tiles
    me, n_chip = me_ref[0], n_row // 2
    valid = iota(slots, 1) < count_ref[0]
    _, rank_row, rank_col = ranks(cols, valid, blocks, row_tiles)
    cols_c, rows_c = flip(cols, slots), flip(rows, slots)
    valid_c = iota(slots, 0) < count_ref[0]
    slot_c = jnp.sum(jnp.where(cols_c == iota(blocks, 1), rank_row, 0), axis=1, keepdims=True)
    slot_r = jnp.sum(jnp.where(cols == iota(blocks, 0), rank_col, 0), axis=0, keepdims=True)

    def away(c, s):
        owner = c // row_tiles
        return ((owner >> 1) ^ (me >> 1)) * (2 * SLOT) + (owner & 1) * SLOT + s

    away_r, away_c = away(cols, slot_r), away(cols_c, slot_c)
    per = 2 * SLOT
    chip, chip_c = cols // row_tiles >> 1 == me >> 1, cols_c // row_tiles >> 1 == me >> 1
    near, near_c = valid & chip, valid_c & chip_c
    far, far_c = valid & ~chip, valid_c & ~chip_c
    write_list(
        out_ref, 0, rows, rows_c, near, near_c, row_tiles, cols_c % (2 * row_tiles), 2 * row_tiles
    )
    write_list(
        out_ref, 1, rows, rows_c, far, far_c, row_tiles, away_c - per, (n_chip - 1) * per
    )
    own, own_c = valid & (cols // row_tiles == me), valid_c & (cols_c // row_tiles == me)
    other, other_c = valid & (cols // row_tiles != me), valid_c & (cols_c // row_tiles != me)
    write_list(out_ref, 2, away_r, away_c, other, other_c, n_chip * per, rows_c, row_tiles)
    write_list(
        out_ref, 3, cols % row_tiles, cols_c % row_tiles, own, own_c, row_tiles, rows_c, row_tiles
    )


def sparse_loop(list_ref, which, x_ref, tiles_ref, acc_ref, forward):
    def step(s, carry):
        for u in range(UNROLL):
            p = 2 * (s * UNROLL + u)
            w0 = list_ref[which, p]
            w1 = list_ref[which, p + 1]
            x = jnp.concatenate([x_ref[(w0 >> 10) & 1023], x_ref[(w1 >> 10) & 1023]], axis=1)
            t0, t1 = tiles_ref[w0 & 1023], tiles_ref[w1 & 1023]
            if forward:
                part = lax.dot_general(
                    x,
                    jnp.concatenate([t0, t1], axis=1),
                    (((1,), (1,)), ((), ())),
                    preferred_element_type=F32,
                )
            else:
                part = jnp.dot(x, jnp.concatenate([t0, t1], axis=0), preferred_element_type=F32)
            acc_ref[w0 >> 20] += part
        return carry

    lax.fori_loop(0, list_ref[4 + which, 0], step, 0)


def load_kernel(in_ref, out_ref, sems):
    n = in_ref.shape[0] // LOADS
    copies = [
        pltpu.make_async_copy(
            in_ref.at[pl.ds(i * n, n)], out_ref.at[pl.ds(i * n, n)], sems.at[i]
        )
        for i in range(LOADS)
    ]
    for c in copies:
        c.start()
    for c in copies:
        c.wait()


def pack_kernel(me_ref, feat_ref, sib_ref, out_ref):
    tiles = feat_ref.shape[1] // TILE
    base = (me_ref[0] & 1) * tiles
    for k in range(tiles):
        out_ref[base + k] = feat_ref[:, k * TILE : (k + 1) * TILE]
        out_ref[tiles - base + k] = sib_ref[:, k * TILE : (k + 1) * TILE]
    out_ref[2 * tiles] = jnp.zeros_like(out_ref[0])


def send_kernel(n_chip, row_tiles, me_ref, *refs):
    need_refs, x_ref, outs = refs[: n_chip - 1], refs[n_chip - 1], refs[n_chip:]
    for need_ref, out in zip(need_refs, outs):
        for q in range(2):
            for j in range(SLOT):
                out[q * SLOT + j] = x_ref[
                    q * row_tiles + need_ref[((me_ref[0] >> 1) << 1) + q, j]
                ]


def fill_from_wide(x_ref, wide_ref, count):
    for k in range(count):
        x_ref[k] = wide_ref[:, k * TILE : (k + 1) * TILE]
    x_ref[count] = jnp.zeros_like(x_ref[count])


def near_fwd_kernel(list_ref, tiles_ref, x_ref, acc_ref):
    acc_ref[...] = jnp.zeros_like(acc_ref)
    sparse_loop(list_ref, 0, x_ref, tiles_ref, acc_ref, True)


def own_bwd_kernel(list_ref, tiles_ref, wide_ref, acc_ref, x_ref):
    fill_from_wide(x_ref, wide_ref, x_ref.shape[0] - 1)
    acc_ref[...] = jnp.zeros_like(acc_ref)
    sparse_loop(list_ref, 3, x_ref, tiles_ref, acc_ref, False)


def far_fwd_kernel(n_in, list_ref, me_ref, tiles_ref, *refs):
    ins, base_ref, rest = refs[:n_in][::-1], refs[n_in], refs[n_in + 1 :]
    outs, (x_ref, acc_ref) = rest[:-2], rest[-2:]
    per = 2 * SLOT
    for d, r in enumerate(ins):
        x_ref[d * per : (d + 1) * per] = r[...]
    x_ref[n_in * per] = jnp.zeros_like(x_ref[0])
    acc_ref[...] = base_ref[...]
    sparse_loop(list_ref, 1, x_ref, tiles_ref, acc_ref, True)
    per = acc_ref.shape[0] // len(outs)
    for k, out in enumerate(outs):
        block = me_ref[0] ^ k
        for i in range(per):
            out[:, i * TILE : (i + 1) * TILE] = acc_ref[block * per + i].astype(BF)


def weight_kernel(me_ref, own_ref, sib_ref, keep_ref, *outs):
    n_f = own_ref.shape[0] - keep_ref.shape[1]
    per = keep_ref.shape[0]
    core = me_ref[0] & 1
    pairs = [(r, r[n_f:, :]) for r in (own_ref, sib_ref)]
    for e in range(len(outs) + 1):
        row = ((((me_ref[0] >> 1) ^ e) << 1) + core) * per
        rows = pl.ds(pl.multiple_of(row, per), per)
        total = sum(
            lax.dot_general(r[rows, :], z, (((1,), (1,)), ((), ())), preferred_element_type=F32)
            for r, z in pairs
        )
        if e == 0:
            keep_ref[...] = total
        else:
            outs[e - 1][...] = total.astype(BF)


def far_bwd_kernel(n_col, list_ref, mec_ref, mer_ref, tiles_ref, *refs):
    ins, rest = refs[:n_col], refs[n_col:]
    wide_ref, sib_ref, (x_ref, acc_ref) = rest[0], rest[1], rest[-2:]
    outs = rest[2:-2]
    per = 2 * SLOT
    gather_blocks(wide_ref, mec_ref[0], ins[::-1])
    fill_from_wide(x_ref, wide_ref, x_ref.shape[0] - 1)
    acc_ref[...] = jnp.zeros_like(acc_ref)
    sparse_loop(list_ref, 2, x_ref, tiles_ref, acc_ref, False)
    for e, out in enumerate(outs):
        out[...] = acc_ref[(e + 1) * per : (e + 2) * per].astype(BF)
    other = 1 - (mer_ref[0] & 1)
    for j in range(SLOT):
        sib_ref[j] = acc_ref[other * SLOT + j].astype(BF)


def forward_kernel(me_ref, *refs):
    other = 1 - (me_ref[0] & 1)
    for e, r in enumerate(refs[:-1][::-1]):
        for j in range(SLOT):
            refs[-1][e * SLOT + j] = r[other * SLOT + j]


def join_kernel(n_chip, me_ref, table_ref, base_ref, sib_ref, fwd_ref, *refs):
    ins, (out_ref, acc_ref) = refs[:-2][::-1], refs[-2:]
    me = me_ref[0]
    core = me & 1
    n_row = 2 * n_chip

    def tile(e, j, other):
        return table_ref[(other * n_chip + e) * n_row + me, j]

    acc_ref[...] = base_ref[...]
    for j in range(SLOT):
        acc_ref[tile(0, j, 1)] += sib_ref[j].astype(F32)
        for e, r in enumerate(ins):
            acc_ref[tile(e + 1, j, 0)] += r[core * SLOT + j].astype(F32)
            acc_ref[tile(e + 1, j, 1)] += fwd_ref[e * SLOT + j].astype(F32)
    for k in range(acc_ref.shape[0]):
        out_ref[:, k * TILE : (k + 1) * TILE] = acc_ref[k].astype(BF)


def pair_kernel(me_ref, own_ref, sib_ref, out_ref):
    core = me_ref[0] & 1
    out_ref[core] = own_ref[...]
    out_ref[1 - core] = sib_ref[...]


def weight_place_kernel(me_ref, *refs):
    out_ref = refs[-1]
    per = refs[0].shape[1]
    for e, r in enumerate(refs[:-1]):
        for q in range(2):
            row = (((me_ref[0] >> 1) ^ e) << 1) + q
            out_ref[pl.ds(pl.multiple_of(row * per, per), per), :] = r[q]


def dense_kernel(n_col, me_ref, wt_ref, w_ref, *refs):
    s_refs, g_refs = refs[:n_col][::-1], refs[n_col : 2 * n_col][::-1]
    o_refs, y_refs = refs[2 * n_col : 3 * n_col], refs[3 * n_col : 4 * n_col]
    sz_ref = refs[4 * n_col]
    f_loc = s_refs[0].shape[0]
    n_f = f_loc * n_col
    s_ref, z_ref = sz_ref.at[pl.ds(0, n_f)], sz_ref.at[pl.ds(n_f, sz_ref.shape[0] - n_f)]
    me = me_ref[0]
    for k in range(n_col):
        s_ref[pl.ds(pl.multiple_of((me ^ k) * f_loc, f_loc), f_loc), :] = s_refs[k][...]
    s_all = s_ref[...]
    for k in range(n_col):
        rows = pl.ds(pl.multiple_of((me ^ k) * f_loc, f_loc), f_loc)
        pre = jnp.dot(wt_ref[rows, :], s_all, preferred_element_type=F32)
        sig = 1.0 / (1.0 + jnp.exp(-pre))
        o_refs[k][...] = (pre * sig).astype(BF)
        slope = sig * (1.0 + pre * (1.0 - sig))
        z_ref[rows, :] = (g_refs[k][...].astype(F32) * slope).astype(BF)
    z_all = z_ref[...]
    for k in range(n_col):
        rows = pl.ds(pl.multiple_of((me ^ k) * f_loc, f_loc), f_loc)
        y_refs[k][...] = jnp.dot(w_ref[rows, :], z_all, preferred_element_type=F32).astype(BF)


def gather_blocks(wide_ref, me, refs):
    width = refs[0].shape[1]
    for k, r in enumerate(refs):
        wide_ref[:, pl.ds(pl.multiple_of((me ^ k) * width, width), width)] = r[...]


def place_kernel(me_ref, *refs):
    wide_ref = refs[-1]
    width = refs[0].shape[1]
    for k, r in enumerate(refs[:-1]):
        at = pl.multiple_of((me_ref[0] ^ k) * width, width)
        wide_ref[:, pl.ds(at, width)] = r[: wide_ref.shape[0], :]


def turn_kernel(x_ref, out_ref):
    out_ref[...] = x_ref[...].T


def split_kernel(me_ref, x_ref, *outs):
    width = outs[0].shape[1]
    for k, out in enumerate(outs):
        out[...] = x_ref[:, pl.ds(pl.multiple_of((me_ref[0] ^ k) * width, width), width)]


def weight_cols_kernel(n_chip, me_ref, *refs):
    n_col = (len(refs) - n_chip - 2) // 2
    ins, o_refs = refs[:n_chip], refs[n_chip : n_chip + n_col]
    outs, own_ref, sum_ref = refs[n_chip + n_col : -2], refs[-2], refs[-1]
    total = ins[0][...]
    for r in ins[1:]:
        total += r[...].astype(F32)
    sum_ref[...] = total
    h_loc, part = o_refs[0].shape
    rows = total.shape[0] * h_loc // part
    for k, out in enumerate(outs):
        if k:
            out[:h_loc, :] = o_refs[k][...]
        for c in range(n_col):

            @pl.when(me_ref[0] ^ k == c)
            def _():
                mine = sum_ref[:, c * h_loc : (c + 1) * h_loc]
                if k == 0:
                    own_ref[...] = mine
                else:
                    for i in range(part // h_loc):
                        out[h_loc : h_loc + rows, i * h_loc : (i + 1) * h_loc] = mine[
                            i * rows : (i + 1) * rows
                        ].astype(BF)


def weight_scale_kernel(scale, own_ref, *refs):
    out_ref = refs[-1]
    n_rows, h_loc = own_ref.shape
    rows = n_rows * h_loc // refs[0].shape[1]
    for i in range(n_rows // rows):
        total = own_ref[i * rows : (i + 1) * rows, :]
        for r in refs[:-1]:
            total += r[h_loc : h_loc + rows, i * h_loc : (i + 1) * h_loc].astype(F32)
        out_ref[i * rows : (i + 1) * rows, :] = total * scale


def shards(features, weight, tile_cols, tile_rows, tile_count, tile_values, out_grad):
    n_row, n_col = lax.axis_size("row"), lax.axis_size("col")
    n_chip = n_row // 2
    me_r, me_c = lax.axis_index("row").astype(jnp.int32), lax.axis_index("col").astype(jnp.int32)
    mer, mec = me_r.reshape(1), me_c.reshape(1)
    f_loc, nodes = features.shape
    h_loc = out_grad.shape[0]
    n_f, n_h = weight.shape
    row_tiles = nodes // TILE
    part = nodes // n_col
    slots = tile_cols.shape[1]
    per = 2 * SLOT
    sds = jax.ShapeDtypeStruct
    tile_flops = 2 * f_loc * TILE * TILE
    tile_bytes = slots * TILE * TILE * 2

    def over_chips(x):
        return swap(x, "row", n_row, 1)

    sib_feat = over_chips(features)
    need = call(
        functools.partial(need_kernel, n_row, row_tiles),
        sds((n_row, 128), jnp.int32),
        [],
        (tile_count,),
        (tile_cols,),
    )
    mer, mec, need = lax.optimization_barrier((mer, mec, need))
    needs = [need] + [swap(need, "row", n_row, 2 * e) for e in range(1, n_chip)]
    length = -(-(slots + n_chip * per + 2 * UNROLL) // 128) * 128
    x_near = call(
        pack_kernel,
        sds((2 * row_tiles + 1, f_loc, TILE), BF),
        [],
        (mer,),
        (features, sib_feat),
        nbytes=f_loc * nodes * 8,
    )
    tile_values, mer, mec = lax.optimization_barrier((tile_values, mer, mec))
    tile_values = pl.pallas_call(
        load_kernel,
        out_shape=sds(tile_values.shape, BF),
        in_specs=[pl.BlockSpec(memory_space=pltpu.HBM)],
        out_specs=VM,
        scratch_shapes=[pltpu.SemaphoreType.DMA((LOADS,))],
        compiler_params=pltpu.CompilerParams(vmem_limit_bytes=24 << 20),
        cost_estimate=pl.CostEstimate(flops=0, bytes_accessed=tile_bytes, transcendentals=0),
    )(pltpu.with_memory_space_constraint(tile_values, pltpu.HBM))
    needs, x_near, tile_values = lax.optimization_barrier((needs, x_near, tile_values))
    sends = call(
        functools.partial(send_kernel, n_chip, row_tiles),
        [sds((per, f_loc, TILE), BF)] * (n_chip - 1),
        [],
        (mer, *needs[1:]),
        (x_near,),
        nbytes=4 * n_chip * per * f_loc * TILE,
    )
    got = [swap(x, "row", n_row, 2 * (e + 1)) for e, x in enumerate(sends)]
    needs, sends, lists_in, out_grad = lax.optimization_barrier(
        (needs, sends, (tile_cols, tile_rows), out_grad)
    )
    lists = call(
        functools.partial(lists_kernel, n_row, row_tiles),
        sds((8, length), jnp.int32),
        [],
        (tile_count, mer),
        lists_in,
    )
    table = jnp.concatenate(needs, axis=0)
    table = jnp.concatenate([table, over_chips(table)], axis=0)
    got, table = lax.optimization_barrier((got[::-1], table))

    g_parts = call(
        split_kernel,
        [sds((h_loc, part), BF)] * n_col,
        [],
        (mec,),
        (out_grad,),
        nbytes=h_loc * nodes * 4,
    )
    grads = [g if k == 0 else swap(g, "col", n_col, k) for k, g in enumerate(g_parts)]

    acc = call(
        near_fwd_kernel,
        sds((row_tiles, f_loc, TILE), F32),
        [],
        (lists,),
        (x_near,),
        (tile_values,),
        flops=tile_flops * slots,
        nbytes=tile_bytes,
    )
    s_parts = call(
        functools.partial(far_fwd_kernel, n_chip - 1),
        [sds((f_loc, part), BF)] * n_col,
        [
            pltpu.VMEM(((n_chip - 1) * per + 1, f_loc, TILE), BF),
            pltpu.VMEM((row_tiles, f_loc, TILE), F32),
        ],
        (lists, mec),
        (*got, acc),
        (tile_values,),
        flops=tile_flops * slots,
        nbytes=tile_bytes,
    )
    s_got = [s if k == 0 else swap(s, "col", n_col, k) for k, s in enumerate(s_parts)]

    weight_t, _ = lax.optimization_barrier((weight, s_parts[0]))
    weight_t = call(turn_kernel, sds((n_h, n_f), BF), [], (), (weight_t,), nbytes=n_f * n_h * 4)
    res = call(
        functools.partial(dense_kernel, n_col),
        [sds((h_loc, part), BF)] * n_col
        + [sds((f_loc, part), BF)] * n_col
        + [sds((n_f + n_h, part), BF)],
        [],
        (mec,),
        (weight_t, weight, *s_got[::-1], *grads[::-1]),
        flops=4 * n_f * n_h * part,
        nbytes=n_f * part * 8,
    )
    o_parts, y_parts, sz = res[:n_col], res[n_col : 2 * n_col], res[-1]
    y_got = [y if k == 0 else swap(y, "col", n_col, k) for k, y in enumerate(y_parts)]

    w_rows = n_f // n_row
    w_parts = call(
        weight_kernel,
        [sds((w_rows, n_h), F32)] + [sds((w_rows, n_h), BF)] * (n_chip - 1),
        [],
        (mer,),
        (sz, over_chips(sz)),
        flops=2 * n_f * n_h * part,
        nbytes=n_f * part * 8,
    )
    w_chips = [w if e == 0 else swap(w, "row", n_row, 2 * e) for e, w in enumerate(w_parts)]
    more = -(-(w_rows * h_loc // part) // 16) * 16
    mixed = call(
        functools.partial(weight_cols_kernel, n_chip),
        [sds((h_loc + more, part), BF)] * n_col + [sds((w_rows, h_loc), F32)],
        [pltpu.VMEM((w_rows, n_h), F32)],
        (mec,),
        (*w_chips, *o_parts),
        nbytes=n_h * part * 4,
    )
    w_own_cols = mixed[-1]
    mixed = [m if k == 0 else swap(m, "col", n_col, k) for k, m in enumerate(mixed[:-1])]

    y_got, w_chips = lax.optimization_barrier((y_got[::-1], w_chips))
    back = call(
        functools.partial(far_bwd_kernel, n_col),
        [sds((f_loc, nodes), BF), sds((SLOT, f_loc, TILE), BF)]
        + [sds((per, f_loc, TILE), BF)] * (n_chip - 1),
        [
            pltpu.VMEM((row_tiles + 1, f_loc, TILE), BF),
            pltpu.VMEM((n_chip * per, f_loc, TILE), F32),
        ],
        (lists, mec, mer),
        tuple(y_got),
        (tile_values,),
        flops=tile_flops * slots,
        nbytes=tile_bytes,
    )
    y_wide, to_sib, contribs = back[0], back[1], back[2:]
    returned = [swap(x, "row", n_row, 2 * (e + 1)) for e, x in enumerate(contribs)]
    from_sib = over_chips(to_sib)

    w_mine = call(
        functools.partial(weight_scale_kernel, float(nodes * n_row) ** (-0.5)),
        sds((w_rows, h_loc), F32),
        [],
        (),
        (w_own_cols, *mixed[:0:-1]),
    )

    acc_b = call(
        own_bwd_kernel,
        sds((row_tiles, f_loc, TILE), F32),
        [pltpu.VMEM((row_tiles + 1, f_loc, TILE), BF)],
        (lists,),
        (y_wide,),
        (tile_values,),
        flops=tile_flops * slots,
        nbytes=tile_bytes,
    )
    returned, acc_b, w_mine = lax.optimization_barrier((returned[::-1], acc_b, w_mine))
    passed = call(
        forward_kernel,
        sds(((n_chip - 1) * SLOT, f_loc, TILE), BF),
        [],
        (mer,),
        tuple(returned),
    )
    w_pair = call(
        pair_kernel, sds((2, w_rows, h_loc), F32), [], (mer,), (w_mine, over_chips(w_mine))
    )
    w_chips = [w_pair] + [swap(w_pair, "row", n_row, 2 * e) for e in range(1, n_chip)]

    input_grad = call(
        functools.partial(join_kernel, n_chip),
        sds((f_loc, nodes), BF),
        [pltpu.VMEM((row_tiles, f_loc, TILE), F32)],
        (mer, table),
        (acc_b, from_sib, over_chips(passed), *returned),
        nbytes=f_loc * nodes * 8,
    )
    w_chips, input_grad = lax.optimization_barrier((w_chips, input_grad))
    weight_grad = call(
        weight_place_kernel,
        sds((n_f, h_loc), F32),
        [],
        (mer,),
        tuple(w_chips),
        nbytes=n_f * h_loc * 8,
    )
    output = call(
        place_kernel, sds((h_loc, nodes), BF), [], (mec,), (o_parts[0], *mixed[1:]), nbytes=h_loc * nodes * 4
    )
    return output, input_grad, weight_grad


def solution(mesh):
    return jax.shard_map(
        shards,
        mesh=mesh,
        in_specs=(
            P("col", "row"),
            P(),
            P("row", None),
            P("row", None),
            P("row"),
            P("row", None, None),
            P("col", "row"),
        ),
        out_specs=(P("col", "row"), P("col", "row"), P(None, "col")),
        check_vma=False,
    )
```

```python
import functools

import jax
import jax.numpy as jnp
from jax import lax
from jax.experimental import pallas as pl
from jax.experimental.pallas import tpu as pltpu
from jax.sharding import PartitionSpec as P

TILE = 128
SLOT = 4
UNROLL = 8
LOADS = 8
BF = jnp.bfloat16
F32 = jnp.float32
VM = pl.BlockSpec(memory_space=pltpu.VMEM)
SM = pl.BlockSpec(memory_space=pltpu.SMEM)


def call(kernel, outs, scratch, smem, vmem, held=(), flops=0, nbytes=0, limit=24):
    return pl.pallas_call(
        kernel,
        out_shape=outs,
        in_specs=[SM] * len(smem) + [VM] * len(held) + [VM] * len(vmem),
        out_specs=jax.tree.map(lambda _: VM, outs),
        scratch_shapes=scratch,
        compiler_params=pltpu.CompilerParams(vmem_limit_bytes=limit << 20),
        cost_estimate=pl.CostEstimate(flops=flops, bytes_accessed=nbytes, transcendentals=0),
    )(*[pltpu.with_memory_space_constraint(x, pltpu.SMEM) for x in smem], *held, *vmem)


def swap(x, axis, n, k):
    return lax.ppermute(x, axis, [(i, i ^ k) for i in range(n)])


def flip(x, n):
    i = lax.broadcasted_iota(jnp.int32, (n, n), 0)
    j = lax.broadcasted_iota(jnp.int32, (n, n), 1)
    return jnp.sum(jnp.where(i == j, x, 0), axis=1 if x.shape[0] == 1 else 0, keepdims=True)


def iota(n, axis):
    return lax.broadcasted_iota(jnp.int32, (n, 1) if axis == 0 else (1, n), axis)


def ranks(cols, valid, blocks, row_tiles):
    b_col, b_row = iota(blocks, 0), iota(blocks, 1)
    hit = jnp.where((cols == b_col) & valid, 1, 0)
    used_col = jnp.max(hit, axis=1, keepdims=True)
    used_row = flip(used_col, blocks)
    same = (b_col // row_tiles) == (b_row // row_tiles)
    rank_row = jnp.sum(jnp.where(same & (b_col < b_row), used_col, 0), axis=0, keepdims=True)
    rank_col = jnp.sum(jnp.where(same & (b_row < b_col), used_row, 0), axis=1, keepdims=True)
    return used_row, rank_row, rank_col


def need_kernel(n_row, row_tiles, count_ref, cols_ref, need_ref):
    cols = cols_ref[...]
    blocks = n_row * row_tiles
    valid = iota(cols.shape[1], 1) < count_ref[0]
    used, rank, _ = ranks(cols, valid, blocks, row_tiles)
    b = iota(blocks, 1)
    owner = (b // row_tiles) == iota(n_row, 0)
    lane = iota(128, 1)
    total = jnp.zeros((n_row, 128), jnp.int32)
    for j in range(SLOT):
        pick = jnp.where((used > 0) & (rank == j), b % row_tiles, 0)
        total += jnp.where(
            lane == j, jnp.sum(jnp.where(owner, pick, 0), axis=1, keepdims=True), 0
        )
    need_ref[...] = total


def write_list(out_ref, which, key_row, key_col, valid_row, valid_col, groups, source, blank):
    slots, length = key_row.shape[1], out_ref.shape[1]
    t_row, t_col = iota(slots, 1), iota(slots, 0)
    key_row, key_col = jnp.where(valid_row, key_row, -1), jnp.where(valid_col, key_col, -1)
    g_col, g_row = iota(groups, 0), iota(128, 1)
    count = jnp.sum(jnp.where(key_row == g_col, 1, 0), axis=1, keepdims=True)
    even = ((count + 1) >> 1) << 1
    start = jnp.sum(jnp.where(g_col < g_row, even, 0), axis=0, keepdims=True)
    first = jnp.sum(jnp.where(key_col == g_row, start, 0), axis=1, keepdims=True)
    rank = jnp.sum(jnp.where((key_row == key_col) & (t_row < t_col), 1, 0), axis=1, keepdims=True)
    place = jnp.where(valid_col, first + rank, -1)
    word = t_col | (source << 10) | (key_col << 20)
    pad = blank << 10
    words = jnp.sum(jnp.where(place == iota(length, 1), word - pad, 0), axis=0, keepdims=True) + pad
    out_ref[which : which + 1, :] = words
    total = jnp.sum(even, axis=0, keepdims=True)
    steps = (total + (2 * UNROLL - 1)) // (2 * UNROLL)
    out_ref[4 + which : 5 + which, :] = jnp.broadcast_to(steps, (1, length))


def lists_kernel(n_row, row_tiles, count_ref, me_ref, cols_ref, rows_ref, out_ref):
    cols, rows = cols_ref[...], rows_ref[...]
    slots = cols.shape[1]
    blocks = n_row * row_tiles
    me, n_chip = me_ref[0], n_row // 2
    valid = iota(slots, 1) < count_ref[0]
    _, rank_row, rank_col = ranks(cols, valid, blocks, row_tiles)
    cols_c, rows_c = flip(cols, slots), flip(rows, slots)
    valid_c = iota(slots, 0) < count_ref[0]
    slot_c = jnp.sum(jnp.where(cols_c == iota(blocks, 1), rank_row, 0), axis=1, keepdims=True)
    slot_r = jnp.sum(jnp.where(cols == iota(blocks, 0), rank_col, 0), axis=0, keepdims=True)

    def away(c, s):
        owner = c // row_tiles
        return ((owner >> 1) ^ (me >> 1)) * (2 * SLOT) + (owner & 1) * SLOT + s

    away_r, away_c = away(cols, slot_r), away(cols_c, slot_c)
    per = 2 * SLOT
    chip, chip_c = cols // row_tiles >> 1 == me >> 1, cols_c // row_tiles >> 1 == me >> 1
    near, near_c = valid & chip, valid_c & chip_c
    far, far_c = valid & ~chip, valid_c & ~chip_c
    write_list(
        out_ref, 0, rows, rows_c, near, near_c, row_tiles, cols_c % (2 * row_tiles), 2 * row_tiles
    )
    write_list(
        out_ref, 1, rows, rows_c, far, far_c, row_tiles, away_c - per, (n_chip - 1) * per
    )
    own, own_c = valid & (cols // row_tiles == me), valid_c & (cols_c // row_tiles == me)
    other, other_c = valid & (cols // row_tiles != me), valid_c & (cols_c // row_tiles != me)
    write_list(out_ref, 2, away_r, away_c, other, other_c, n_chip * per, rows_c, row_tiles)
    write_list(
        out_ref, 3, cols % row_tiles, cols_c % row_tiles, own, own_c, row_tiles, rows_c, row_tiles
    )


def sparse_loop(list_ref, which, x_ref, tiles_ref, acc_ref, forward):
    def step(s, carry):
        for u in range(UNROLL):
            p = 2 * (s * UNROLL + u)
            w0 = list_ref[which, p]
            w1 = list_ref[which, p + 1]
            x = jnp.concatenate([x_ref[(w0 >> 10) & 1023], x_ref[(w1 >> 10) & 1023]], axis=1)
            t0, t1 = tiles_ref[w0 & 1023], tiles_ref[w1 & 1023]
            if forward:
                part = lax.dot_general(
                    x,
                    jnp.concatenate([t0, t1], axis=1),
                    (((1,), (1,)), ((), ())),
                    preferred_element_type=F32,
                )
            else:
                part = jnp.dot(x, jnp.concatenate([t0, t1], axis=0), preferred_element_type=F32)
            acc_ref[w0 >> 20] += part
        return carry

    lax.fori_loop(0, list_ref[4 + which, 0], step, 0)


def load_kernel(in_ref, out_ref, sems):
    n = in_ref.shape[0] // LOADS
    copies = [
        pltpu.make_async_copy(
            in_ref.at[pl.ds(i * n, n)], out_ref.at[pl.ds(i * n, n)], sems.at[i]
        )
        for i in range(LOADS)
    ]
    for c in copies:
        c.start()
    for c in copies:
        c.wait()


def pack_kernel(me_ref, feat_ref, sib_ref, out_ref):
    tiles = feat_ref.shape[1] // TILE
    base = (me_ref[0] & 1) * tiles
    for k in range(tiles):
        out_ref[base + k] = feat_ref[:, k * TILE : (k + 1) * TILE]
        out_ref[tiles - base + k] = sib_ref[:, k * TILE : (k + 1) * TILE]
    out_ref[2 * tiles] = jnp.zeros_like(out_ref[0])


def send_kernel(n_chip, row_tiles, me_ref, *refs):
    need_refs, x_ref, outs = refs[: n_chip - 1], refs[n_chip - 1], refs[n_chip:]
    for need_ref, out in zip(need_refs, outs):
        for q in range(2):
            for j in range(SLOT):
                out[q * SLOT + j] = x_ref[
                    q * row_tiles + need_ref[((me_ref[0] >> 1) << 1) + q, j]
                ]


def fill_from_wide(x_ref, wide_ref, count):
    for k in range(count):
        x_ref[k] = wide_ref[:, k * TILE : (k + 1) * TILE]
    x_ref[count] = jnp.zeros_like(x_ref[count])


def near_fwd_kernel(list_ref, tiles_ref, x_ref, acc_ref):
    acc_ref[...] = jnp.zeros_like(acc_ref)
    sparse_loop(list_ref, 0, x_ref, tiles_ref, acc_ref, True)


def own_bwd_kernel(list_ref, tiles_ref, wide_ref, acc_ref, x_ref):
    fill_from_wide(x_ref, wide_ref, x_ref.shape[0] - 1)
    acc_ref[...] = jnp.zeros_like(acc_ref)
    sparse_loop(list_ref, 3, x_ref, tiles_ref, acc_ref, False)


def far_fwd_kernel(n_in, list_ref, me_ref, tiles_ref, *refs):
    ins, base_ref, rest = refs[:n_in][::-1], refs[n_in], refs[n_in + 1 :]
    outs, (x_ref, acc_ref) = rest[:-2], rest[-2:]
    per = 2 * SLOT
    for d, r in enumerate(ins):
        x_ref[d * per : (d + 1) * per] = r[...]
    x_ref[n_in * per] = jnp.zeros_like(x_ref[0])
    acc_ref[...] = base_ref[...]
    sparse_loop(list_ref, 1, x_ref, tiles_ref, acc_ref, True)
    per = acc_ref.shape[0] // len(outs)
    for k, out in enumerate(outs):
        block = me_ref[0] ^ k
        for i in range(per):
            out[:, i * TILE : (i + 1) * TILE] = acc_ref[block * per + i].astype(BF)


def weight_kernel(me_ref, own_ref, sib_ref, keep_ref, *outs):
    n_f = own_ref.shape[0] - keep_ref.shape[1]
    per = keep_ref.shape[0]
    core = me_ref[0] & 1
    pairs = [(r, r[n_f:, :]) for r in (own_ref, sib_ref)]
    for e in range(len(outs) + 1):
        row = ((((me_ref[0] >> 1) ^ e) << 1) + core) * per
        rows = pl.ds(pl.multiple_of(row, per), per)
        total = sum(
            lax.dot_general(r[rows, :], z, (((1,), (1,)), ((), ())), preferred_element_type=F32)
            for r, z in pairs
        )
        if e == 0:
            keep_ref[...] = total
        else:
            outs[e - 1][...] = total.astype(BF)


def far_bwd_kernel(n_col, list_ref, mec_ref, mer_ref, tiles_ref, *refs):
    ins, rest = refs[:n_col], refs[n_col:]
    wide_ref, sib_ref, (x_ref, acc_ref) = rest[0], rest[1], rest[-2:]
    outs = rest[2:-2]
    per = 2 * SLOT
    gather_blocks(wide_ref, mec_ref[0], ins[::-1])
    fill_from_wide(x_ref, wide_ref, x_ref.shape[0] - 1)
    acc_ref[...] = jnp.zeros_like(acc_ref)
    sparse_loop(list_ref, 2, x_ref, tiles_ref, acc_ref, False)
    for e, out in enumerate(outs):
        out[...] = acc_ref[(e + 1) * per : (e + 2) * per].astype(BF)
    other = 1 - (mer_ref[0] & 1)
    for j in range(SLOT):
        sib_ref[j] = acc_ref[other * SLOT + j].astype(BF)


def table_kernel(n_row, me_ref, all_ref, out_ref):
    for p in range(out_ref.shape[0]):
        out_ref[p : p + 1, :] = all_ref[pl.ds(p * n_row + me_ref[0], 1), :]


def forward_kernel(me_ref, *refs):
    other = 1 - (me_ref[0] & 1)
    for e, r in enumerate(refs[:-1][::-1]):
        for j in range(SLOT):
            refs[-1][e * SLOT + j] = r[other * SLOT + j]


def join_kernel(n_chip, me_ref, table_ref, base_ref, sib_ref, fwd_ref, *refs):
    ins, (out_ref, acc_ref) = refs[:-2][::-1], refs[-2:]
    core = me_ref[0] & 1

    def tile(e, j, other):
        return table_ref[other * n_chip + e, j]

    acc_ref[...] = base_ref[...]
    for j in range(SLOT):
        acc_ref[tile(0, j, 1)] += sib_ref[j].astype(F32)
        for e, r in enumerate(ins):
            acc_ref[tile(e + 1, j, 0)] += r[core * SLOT + j].astype(F32)
            acc_ref[tile(e + 1, j, 1)] += fwd_ref[e * SLOT + j].astype(F32)
    for k in range(acc_ref.shape[0]):
        out_ref[:, k * TILE : (k + 1) * TILE] = acc_ref[k].astype(BF)


def pair_kernel(me_ref, own_ref, sib_ref, out_ref):
    core = me_ref[0] & 1
    out_ref[core] = own_ref[...]
    out_ref[1 - core] = sib_ref[...]


def weight_place_kernel(me_ref, *refs):
    out_ref = refs[-1]
    per = refs[0].shape[1]
    for e, r in enumerate(refs[:-1]):
        for q in range(2):
            row = (((me_ref[0] >> 1) ^ e) << 1) + q
            out_ref[pl.ds(pl.multiple_of(row * per, per), per), :] = r[q]


def dense_kernel(n_col, me_ref, wt_ref, w_ref, *refs):
    s_refs, g_refs = refs[:n_col][::-1], refs[n_col : 2 * n_col][::-1]
    o_refs, y_refs = refs[2 * n_col : 3 * n_col], refs[3 * n_col : 4 * n_col]
    sz_ref = refs[4 * n_col]
    f_loc = s_refs[0].shape[0]
    n_f = f_loc * n_col
    s_ref, z_ref = sz_ref.at[pl.ds(0, n_f)], sz_ref.at[pl.ds(n_f, sz_ref.shape[0] - n_f)]
    me = me_ref[0]
    for k in range(n_col):
        s_ref[pl.ds(pl.multiple_of((me ^ k) * f_loc, f_loc), f_loc), :] = s_refs[k][...]
    s_all = s_ref[...]
    for k in range(n_col):
        rows = pl.ds(pl.multiple_of((me ^ k) * f_loc, f_loc), f_loc)
        pre = jnp.dot(wt_ref[rows, :], s_all, preferred_element_type=F32)
        sig = 1.0 / (1.0 + jnp.exp(-pre))
        o_refs[k][...] = (pre * sig).astype(BF)
        slope = sig * (1.0 + pre * (1.0 - sig))
        z_ref[rows, :] = (g_refs[k][...].astype(F32) * slope).astype(BF)
    z_all = z_ref[...]
    for k in range(n_col):
        rows = pl.ds(pl.multiple_of((me ^ k) * f_loc, f_loc), f_loc)
        y_refs[k][...] = jnp.dot(w_ref[rows, :], z_all, preferred_element_type=F32).astype(BF)


def gather_blocks(wide_ref, me, refs):
    width = refs[0].shape[1]
    for k, r in enumerate(refs):
        wide_ref[:, pl.ds(pl.multiple_of((me ^ k) * width, width), width)] = r[...]


def place_kernel(me_ref, *refs):
    wide_ref = refs[-1]
    width = refs[0].shape[1]
    parts = [refs[0], *refs[-2:0:-1]]
    for k, r in enumerate(parts):
        at = pl.multiple_of((me_ref[0] ^ k) * width, width)
        wide_ref[:, pl.ds(at, width)] = r[: wide_ref.shape[0], :]


def turn_kernel(x_ref, out_ref):
    out_ref[...] = x_ref[...].T


def split_kernel(me_ref, x_ref, *outs):
    width = outs[0].shape[1]
    for k, out in enumerate(outs):
        out[...] = x_ref[:, pl.ds(pl.multiple_of((me_ref[0] ^ k) * width, width), width)]


def weight_cols_kernel(n_chip, me_ref, *refs):
    n_col = (len(refs) - n_chip - 2) // 2
    ins, o_refs = refs[:n_chip], refs[n_chip : n_chip + n_col]
    outs, own_ref, sum_ref = refs[n_chip + n_col : -2], refs[-2], refs[-1]
    total = ins[0][...]
    for r in ins[1:]:
        total += r[...].astype(F32)
    sum_ref[...] = total
    h_loc, part = o_refs[0].shape
    rows = total.shape[0] * h_loc // part
    for k, out in enumerate(outs):
        if k:
            out[:h_loc, :] = o_refs[k][...]
        for c in range(n_col):

            @pl.when(me_ref[0] ^ k == c)
            def _():
                mine = sum_ref[:, c * h_loc : (c + 1) * h_loc]
                if k == 0:
                    own_ref[...] = mine
                else:
                    for i in range(part // h_loc):
                        out[h_loc : h_loc + rows, i * h_loc : (i + 1) * h_loc] = mine[
                            i * rows : (i + 1) * rows
                        ].astype(BF)


def weight_scale_kernel(scale, own_ref, *refs):
    out_ref = refs[-1]
    n_rows, h_loc = own_ref.shape
    rows = n_rows * h_loc // refs[0].shape[1]
    for i in range(n_rows // rows):
        total = own_ref[i * rows : (i + 1) * rows, :]
        for r in refs[:-1]:
            total += r[h_loc : h_loc + rows, i * h_loc : (i + 1) * h_loc].astype(F32)
        out_ref[i * rows : (i + 1) * rows, :] = total * scale


def shards(features, weight, tile_cols, tile_rows, tile_count, tile_values, out_grad):
    n_row, n_col = lax.axis_size("row"), lax.axis_size("col")
    n_chip = n_row // 2
    me_r, me_c = lax.axis_index("row").astype(jnp.int32), lax.axis_index("col").astype(jnp.int32)
    mer, mec = me_r.reshape(1), me_c.reshape(1)
    f_loc, nodes = features.shape
    h_loc = out_grad.shape[0]
    n_f, n_h = weight.shape
    row_tiles = nodes // TILE
    part = nodes // n_col
    slots = tile_cols.shape[1]
    per = 2 * SLOT
    sds = jax.ShapeDtypeStruct
    tile_flops = 2 * f_loc * TILE * TILE
    tile_bytes = slots * TILE * TILE * 2

    def over_chips(x):
        return swap(x, "row", n_row, 1)

    sib_feat = over_chips(features)
    need = call(
        functools.partial(need_kernel, n_row, row_tiles),
        sds((n_row, 128), jnp.int32),
        [],
        (tile_count,),
        (tile_cols,),
    )
    mer, mec, need = lax.optimization_barrier((mer, mec, need))
    needs = [need] + [swap(need, "row", n_row, 2 * e) for e in range(1, n_chip)]
    length = -(-(slots + n_chip * per + 2 * UNROLL) // 128) * 128
    x_near = call(
        pack_kernel,
        sds((2 * row_tiles + 1, f_loc, TILE), BF),
        [],
        (mer,),
        (features, sib_feat),
        nbytes=f_loc * nodes * 8,
    )
    tile_values, mer, mec = lax.optimization_barrier((tile_values, mer, mec))
    tile_values = pl.pallas_call(
        load_kernel,
        out_shape=sds(tile_values.shape, BF),
        in_specs=[pl.BlockSpec(memory_space=pltpu.HBM)],
        out_specs=VM,
        scratch_shapes=[pltpu.SemaphoreType.DMA((LOADS,))],
        compiler_params=pltpu.CompilerParams(vmem_limit_bytes=24 << 20),
        cost_estimate=pl.CostEstimate(flops=0, bytes_accessed=tile_bytes, transcendentals=0),
    )(pltpu.with_memory_space_constraint(tile_values, pltpu.HBM))
    needs, x_near, tile_values = lax.optimization_barrier((needs, x_near, tile_values))
    sends = call(
        functools.partial(send_kernel, n_chip, row_tiles),
        [sds((per, f_loc, TILE), BF)] * (n_chip - 1),
        [],
        (mer, *needs[1:]),
        (x_near,),
        nbytes=4 * n_chip * per * f_loc * TILE,
    )
    got = [swap(x, "row", n_row, 2 * (e + 1)) for e, x in enumerate(sends)]
    needs, sends, lists_in, out_grad = lax.optimization_barrier(
        (needs, sends, (tile_cols, tile_rows), out_grad)
    )
    lists = call(
        functools.partial(lists_kernel, n_row, row_tiles),
        sds((8, length), jnp.int32),
        [],
        (tile_count, mer),
        lists_in,
    )
    table = jnp.concatenate(needs, axis=0)
    table = jnp.concatenate([table, over_chips(table)], axis=0)
    table = call(
        functools.partial(table_kernel, n_row), sds((n_row, 128), jnp.int32), [], (mer,), (table,)
    )
    got, table = lax.optimization_barrier((got, table))

    g_parts = call(
        split_kernel,
        [sds((h_loc, part), BF)] * n_col,
        [],
        (mec,),
        (out_grad,),
        nbytes=h_loc * nodes * 4,
    )
    grads = [g if k == 0 else swap(g, "col", n_col, k) for k, g in enumerate(g_parts)]

    acc = call(
        near_fwd_kernel,
        sds((row_tiles, f_loc, TILE), F32),
        [],
        (lists,),
        (x_near,),
        (tile_values,),
        flops=tile_flops * slots,
        nbytes=tile_bytes,
    )
    s_parts = call(
        functools.partial(far_fwd_kernel, n_chip - 1),
        [sds((f_loc, part), BF)] * n_col,
        [
            pltpu.VMEM(((n_chip - 1) * per + 1, f_loc, TILE), BF),
            pltpu.VMEM((row_tiles, f_loc, TILE), F32),
        ],
        (lists, mec),
        (*got[::-1], acc),
        (tile_values,),
        flops=tile_flops * slots,
        nbytes=tile_bytes,
    )
    s_got = [s if k == 0 else swap(s, "col", n_col, k) for k, s in enumerate(s_parts)]

    weight_t, _ = lax.optimization_barrier((weight, s_parts[0]))
    weight_t = call(turn_kernel, sds((n_h, n_f), BF), [], (), (weight_t,), nbytes=n_f * n_h * 4)
    res = call(
        functools.partial(dense_kernel, n_col),
        [sds((h_loc, part), BF)] * n_col
        + [sds((f_loc, part), BF)] * n_col
        + [sds((n_f + n_h, part), BF)],
        [],
        (mec,),
        (weight_t, weight, *s_got[::-1], *grads[::-1]),
        flops=4 * n_f * n_h * part,
        nbytes=n_f * part * 8,
    )
    o_parts, y_parts, sz = res[:n_col], res[n_col : 2 * n_col], res[-1]
    y_got = [y if k == 0 else swap(y, "col", n_col, k) for k, y in enumerate(y_parts)]

    w_rows = n_f // n_row
    w_parts = call(
        weight_kernel,
        [sds((w_rows, n_h), F32)] + [sds((w_rows, n_h), BF)] * (n_chip - 1),
        [],
        (mer,),
        (sz, over_chips(sz)),
        flops=2 * n_f * n_h * part,
        nbytes=n_f * part * 8,
    )
    w_chips = [w if e == 0 else swap(w, "row", n_row, 2 * e) for e, w in enumerate(w_parts)]
    more = -(-(w_rows * h_loc // part) // 16) * 16
    mixed = call(
        functools.partial(weight_cols_kernel, n_chip),
        [sds((h_loc + more, part), BF)] * n_col + [sds((w_rows, h_loc), F32)],
        [pltpu.VMEM((w_rows, n_h), F32)],
        (mec,),
        (w_chips[0], *w_chips[:0:-1], *o_parts),
        nbytes=n_h * part * 4,
    )
    w_own_cols = mixed[-1]
    mixed = [m if k == 0 else swap(m, "col", n_col, k) for k, m in enumerate(mixed[:-1])]

    y_got, _ = lax.optimization_barrier((y_got[::-1], w_chips[::-1]))
    back = call(
        functools.partial(far_bwd_kernel, n_col),
        [sds((f_loc, nodes), BF), sds((SLOT, f_loc, TILE), BF)]
        + [sds((per, f_loc, TILE), BF)] * (n_chip - 1),
        [
            pltpu.VMEM((row_tiles + 1, f_loc, TILE), BF),
            pltpu.VMEM((n_chip * per, f_loc, TILE), F32),
        ],
        (lists, mec, mer),
        tuple(y_got),
        (tile_values,),
        flops=tile_flops * slots,
        nbytes=tile_bytes,
    )
    y_wide, to_sib, contribs = back[0], back[1], back[2:]
    returned = [swap(x, "row", n_row, 2 * (e + 1)) for e, x in enumerate(contribs)]
    from_sib = over_chips(to_sib)

    w_mine = call(
        functools.partial(weight_scale_kernel, float(nodes * n_row) ** (-0.5)),
        sds((w_rows, h_loc), F32),
        [],
        (),
        (w_own_cols, *mixed[:0:-1]),
    )

    acc_b = call(
        own_bwd_kernel,
        sds((row_tiles, f_loc, TILE), F32),
        [pltpu.VMEM((row_tiles + 1, f_loc, TILE), BF)],
        (lists,),
        (y_wide,),
        (tile_values,),
        flops=tile_flops * slots,
        nbytes=tile_bytes,
    )
    returned, acc_b, w_mine = lax.optimization_barrier((returned[::-1], acc_b, w_mine))
    passed = call(
        forward_kernel,
        sds(((n_chip - 1) * SLOT, f_loc, TILE), BF),
        [],
        (mer,),
        tuple(returned),
    )
    output = call(
        place_kernel, sds((h_loc, nodes), BF), [], (mec,), (o_parts[0], *mixed[:0:-1]), nbytes=h_loc * nodes * 4
    )
    w_hop, output = lax.optimization_barrier((over_chips(w_mine), output))
    w_pair = call(pair_kernel, sds((2, w_rows, h_loc), F32), [], (mer,), (w_mine, w_hop))
    w_chips = [w_pair] + [swap(w_pair, "row", n_row, 2 * e) for e in range(1, n_chip)]

    input_grad = call(
        functools.partial(join_kernel, n_chip),
        sds((f_loc, nodes), BF),
        [pltpu.VMEM((row_tiles, f_loc, TILE), F32)],
        (mer, table),
        (acc_b, from_sib, over_chips(passed), *returned),
        nbytes=f_loc * nodes * 8,
    )
    w_chips, input_grad = lax.optimization_barrier((w_chips, input_grad))
    weight_grad = call(
        weight_place_kernel,
        sds((n_f, h_loc), F32),
        [],
        (mer,),
        tuple(w_chips),
        nbytes=n_f * h_loc * 8,
    )
    return output, input_grad, weight_grad


def solution(mesh):
    return jax.shard_map(
        shards,
        mesh=mesh,
        in_specs=(
            P("col", "row"),
            P(),
            P("row", None),
            P("row", None),
            P("row"),
            P("row", None, None),
            P("col", "row"),
        ),
        out_specs=(P("col", "row"), P("col", "row"), P(None, "col")),
        check_vma=False,
    )
```

```python
import functools

import jax
import jax.numpy as jnp
from jax import lax
from jax.experimental import pallas as pl
from jax.experimental.pallas import tpu as pltpu
from jax.sharding import PartitionSpec as P

TILE = 128
SLOT = 4
UNROLL = 16
LOADS = 8
BF = jnp.bfloat16
F32 = jnp.float32
VM = pl.BlockSpec(memory_space=pltpu.VMEM)
SM = pl.BlockSpec(memory_space=pltpu.SMEM)


def call(kernel, outs, scratch, smem, vmem, held=(), flops=0, nbytes=0, limit=24):
    return pl.pallas_call(
        kernel,
        out_shape=outs,
        in_specs=[SM] * len(smem) + [VM] * len(held) + [VM] * len(vmem),
        out_specs=jax.tree.map(lambda _: VM, outs),
        scratch_shapes=scratch,
        compiler_params=pltpu.CompilerParams(vmem_limit_bytes=limit << 20),
        cost_estimate=pl.CostEstimate(flops=flops, bytes_accessed=nbytes, transcendentals=0),
    )(*[pltpu.with_memory_space_constraint(x, pltpu.SMEM) for x in smem], *held, *vmem)


def swap(x, axis, n, k):
    return lax.ppermute(x, axis, [(i, i ^ k) for i in range(n)])


def flip(x, n):
    i = lax.broadcasted_iota(jnp.int32, (n, n), 0)
    j = lax.broadcasted_iota(jnp.int32, (n, n), 1)
    return jnp.sum(jnp.where(i == j, x, 0), axis=1 if x.shape[0] == 1 else 0, keepdims=True)


def iota(n, axis):
    return lax.broadcasted_iota(jnp.int32, (n, 1) if axis == 0 else (1, n), axis)


def ranks(cols, valid, blocks, row_tiles):
    b_col, b_row = iota(blocks, 0), iota(blocks, 1)
    hit = jnp.where((cols == b_col) & valid, 1, 0)
    used_col = jnp.max(hit, axis=1, keepdims=True)
    used_row = flip(used_col, blocks)
    same = (b_col // row_tiles) == (b_row // row_tiles)
    rank_row = jnp.sum(jnp.where(same & (b_col < b_row), used_col, 0), axis=0, keepdims=True)
    rank_col = jnp.sum(jnp.where(same & (b_row < b_col), used_row, 0), axis=1, keepdims=True)
    return used_row, rank_row, rank_col


def need_kernel(n_row, row_tiles, count_ref, cols_ref, need_ref):
    cols = cols_ref[...]
    blocks = n_row * row_tiles
    valid = iota(cols.shape[1], 1) < count_ref[0]
    used, rank, _ = ranks(cols, valid, blocks, row_tiles)
    b = iota(blocks, 1)
    owner = (b // row_tiles) == iota(n_row, 0)
    lane = iota(128, 1)
    total = jnp.zeros((n_row, 128), jnp.int32)
    for j in range(SLOT):
        pick = jnp.where((used > 0) & (rank == j), b % row_tiles, 0)
        total += jnp.where(
            lane == j, jnp.sum(jnp.where(owner, pick, 0), axis=1, keepdims=True), 0
        )
    need_ref[...] = total


def write_list(out_ref, which, key_row, key_col, valid_row, valid_col, groups, source, blank):
    slots, length = key_row.shape[1], out_ref.shape[1]
    t_row, t_col = iota(slots, 1), iota(slots, 0)
    key_row, key_col = jnp.where(valid_row, key_row, -1), jnp.where(valid_col, key_col, -1)
    g_col, g_row = iota(groups, 0), iota(128, 1)
    count = jnp.sum(jnp.where(key_row == g_col, 1, 0), axis=1, keepdims=True)
    even = ((count + 1) >> 1) << 1
    start = jnp.sum(jnp.where(g_col < g_row, even, 0), axis=0, keepdims=True)
    first = jnp.sum(jnp.where(key_col == g_row, start, 0), axis=1, keepdims=True)
    rank = jnp.sum(jnp.where((key_row == key_col) & (t_row < t_col), 1, 0), axis=1, keepdims=True)
    place = jnp.where(valid_col, first + rank, -1)
    word = t_col | (source << 10) | (key_col << 20)
    pad = blank << 10
    words = jnp.sum(jnp.where(place == iota(length, 1), word - pad, 0), axis=0, keepdims=True) + pad
    out_ref[which : which + 1, :] = words
    total = jnp.sum(even, axis=0, keepdims=True)
    steps = (total + (2 * UNROLL - 1)) // (2 * UNROLL)
    out_ref[4 + which : 5 + which, :] = jnp.broadcast_to(steps, (1, length))


def lists_kernel(n_row, row_tiles, count_ref, me_ref, cols_ref, rows_ref, out_ref):
    cols, rows = cols_ref[...], rows_ref[...]
    slots = cols.shape[1]
    blocks = n_row * row_tiles
    me, n_chip = me_ref[0], n_row // 2
    valid = iota(slots, 1) < count_ref[0]
    _, rank_row, rank_col = ranks(cols, valid, blocks, row_tiles)
    cols_c, rows_c = flip(cols, slots), flip(rows, slots)
    valid_c = iota(slots, 0) < count_ref[0]
    slot_c = jnp.sum(jnp.where(cols_c == iota(blocks, 1), rank_row, 0), axis=1, keepdims=True)
    slot_r = jnp.sum(jnp.where(cols == iota(blocks, 0), rank_col, 0), axis=0, keepdims=True)

    def away(c, s):
        owner = c // row_tiles
        return ((owner >> 1) ^ (me >> 1)) * (2 * SLOT) + (owner & 1) * SLOT + s

    away_r, away_c = away(cols, slot_r), away(cols_c, slot_c)
    per = 2 * SLOT
    chip, chip_c = cols // row_tiles >> 1 == me >> 1, cols_c // row_tiles >> 1 == me >> 1
    near, near_c = valid & chip, valid_c & chip_c
    far, far_c = valid & ~chip, valid_c & ~chip_c
    write_list(
        out_ref, 0, rows, rows_c, near, near_c, row_tiles, cols_c % (2 * row_tiles), 2 * row_tiles
    )
    write_list(
        out_ref, 1, rows, rows_c, far, far_c, row_tiles, away_c - per, (n_chip - 1) * per
    )
    own, own_c = valid & (cols // row_tiles == me), valid_c & (cols_c // row_tiles == me)
    other, other_c = valid & (cols // row_tiles != me), valid_c & (cols_c // row_tiles != me)
    write_list(out_ref, 2, away_r, away_c, other, other_c, n_chip * per, rows_c, row_tiles)
    write_list(
        out_ref, 3, cols % row_tiles, cols_c % row_tiles, own, own_c, row_tiles, rows_c, row_tiles
    )


def sparse_loop(list_ref, which, x_ref, tiles_ref, acc_ref, forward):
    def step(s, carry):
        for u in range(UNROLL):
            p = 2 * (s * UNROLL + u)
            w0 = list_ref[which, p]
            w1 = list_ref[which, p + 1]
            x = jnp.concatenate([x_ref[(w0 >> 10) & 1023], x_ref[(w1 >> 10) & 1023]], axis=1)
            t0, t1 = tiles_ref[w0 & 1023], tiles_ref[w1 & 1023]
            if forward:
                part = lax.dot_general(
                    x,
                    jnp.concatenate([t0, t1], axis=1),
                    (((1,), (1,)), ((), ())),
                    preferred_element_type=F32,
                )
            else:
                part = jnp.dot(x, jnp.concatenate([t0, t1], axis=0), preferred_element_type=F32)
            acc_ref[w0 >> 20] += part
        return carry

    lax.fori_loop(0, list_ref[4 + which, 0], step, 0)


def load_kernel(in_ref, out_ref, sems):
    n = in_ref.shape[0] // LOADS
    copies = [
        pltpu.make_async_copy(
            in_ref.at[pl.ds(i * n, n)], out_ref.at[pl.ds(i * n, n)], sems.at[i]
        )
        for i in range(LOADS)
    ]
    for c in copies:
        c.start()
    for c in copies:
        c.wait()


def pack_kernel(me_ref, feat_ref, sib_ref, out_ref):
    tiles = feat_ref.shape[1] // TILE
    base = (me_ref[0] & 1) * tiles
    for k in range(tiles):
        out_ref[base + k] = feat_ref[:, k * TILE : (k + 1) * TILE]
        out_ref[tiles - base + k] = sib_ref[:, k * TILE : (k + 1) * TILE]
    out_ref[2 * tiles] = jnp.zeros_like(out_ref[0])


def send_kernel(n_chip, row_tiles, me_ref, *refs):
    need_refs, x_ref, outs = refs[: n_chip - 1], refs[n_chip - 1], refs[n_chip:]
    for need_ref, out in zip(need_refs, outs):
        for q in range(2):
            for j in range(SLOT):
                out[q * SLOT + j] = x_ref[
                    q * row_tiles + need_ref[((me_ref[0] >> 1) << 1) + q, j]
                ]


def fill_from_wide(x_ref, wide_ref, count):
    for k in range(count):
        x_ref[k] = wide_ref[:, k * TILE : (k + 1) * TILE]
    x_ref[count] = jnp.zeros_like(x_ref[count])


def near_fwd_kernel(list_ref, tiles_ref, x_ref, acc_ref):
    acc_ref[...] = jnp.zeros_like(acc_ref)
    sparse_loop(list_ref, 0, x_ref, tiles_ref, acc_ref, True)


def own_bwd_kernel(list_ref, tiles_ref, wide_ref, acc_ref, x_ref):
    fill_from_wide(x_ref, wide_ref, x_ref.shape[0] - 1)
    acc_ref[...] = jnp.zeros_like(acc_ref)
    sparse_loop(list_ref, 3, x_ref, tiles_ref, acc_ref, False)


def far_fwd_kernel(n_in, list_ref, me_ref, tiles_ref, *refs):
    ins, base_ref, rest = refs[:n_in][::-1], refs[n_in], refs[n_in + 1 :]
    outs, (x_ref, acc_ref) = rest[:-2], rest[-2:]
    per = 2 * SLOT
    for d, r in enumerate(ins):
        x_ref[d * per : (d + 1) * per] = r[...]
    x_ref[n_in * per] = jnp.zeros_like(x_ref[0])
    acc_ref[...] = base_ref[...]
    sparse_loop(list_ref, 1, x_ref, tiles_ref, acc_ref, True)
    per = acc_ref.shape[0] // len(outs)
    for k, out in enumerate(outs):
        block = me_ref[0] ^ k
        for i in range(per):
            out[:, i * TILE : (i + 1) * TILE] = acc_ref[block * per + i].astype(BF)


def weight_kernel(me_ref, own_ref, sib_ref, keep_ref, *outs):
    n_f = own_ref.shape[0] - keep_ref.shape[1]
    per = keep_ref.shape[0]
    core = me_ref[0] & 1
    pairs = [(r, r[n_f:, :]) for r in (own_ref, sib_ref)]
    for e in range(len(outs) + 1):
        row = ((((me_ref[0] >> 1) ^ e) << 1) + core) * per
        rows = pl.ds(pl.multiple_of(row, per), per)
        total = sum(
            lax.dot_general(r[rows, :], z, (((1,), (1,)), ((), ())), preferred_element_type=F32)
            for r, z in pairs
        )
        if e == 0:
            keep_ref[...] = total
        else:
            outs[e - 1][...] = total.astype(BF)


def far_bwd_kernel(n_col, list_ref, mec_ref, mer_ref, tiles_ref, *refs):
    ins, rest = refs[:n_col], refs[n_col:]
    wide_ref, sib_ref, (x_ref, acc_ref) = rest[0], rest[1], rest[-2:]
    outs = rest[2:-2]
    per = 2 * SLOT
    gather_blocks(wide_ref, mec_ref[0], ins[::-1])
    fill_from_wide(x_ref, wide_ref, x_ref.shape[0] - 1)
    acc_ref[...] = jnp.zeros_like(acc_ref)
    sparse_loop(list_ref, 2, x_ref, tiles_ref, acc_ref, False)
    for e, out in enumerate(outs):
        out[...] = acc_ref[(e + 1) * per : (e + 2) * per].astype(BF)
    other = 1 - (mer_ref[0] & 1)
    for j in range(SLOT):
        sib_ref[j] = acc_ref[other * SLOT + j].astype(BF)


def table_kernel(n_row, me_ref, all_ref, out_ref):
    for p in range(out_ref.shape[0]):
        out_ref[p : p + 1, :] = all_ref[pl.ds(p * n_row + me_ref[0], 1), :]


def forward_kernel(me_ref, *refs):
    other = 1 - (me_ref[0] & 1)
    for e, r in enumerate(refs[:-1][::-1]):
        for j in range(SLOT):
            refs[-1][e * SLOT + j] = r[other * SLOT + j]


def join_kernel(n_chip, me_ref, table_ref, base_ref, sib_ref, fwd_ref, *refs):
    ins, (out_ref, acc_ref) = refs[:-2][::-1], refs[-2:]
    core = me_ref[0] & 1

    def tile(e, j, other):
        return table_ref[other * n_chip + e, j]

    acc_ref[...] = base_ref[...]
    for j in range(SLOT):
        acc_ref[tile(0, j, 1)] += sib_ref[j].astype(F32)
        for e, r in enumerate(ins):
            acc_ref[tile(e + 1, j, 0)] += r[core * SLOT + j].astype(F32)
            acc_ref[tile(e + 1, j, 1)] += fwd_ref[e * SLOT + j].astype(F32)
    for k in range(acc_ref.shape[0]):
        out_ref[:, k * TILE : (k + 1) * TILE] = acc_ref[k].astype(BF)


def pair_kernel(me_ref, own_ref, sib_ref, out_ref):
    core = me_ref[0] & 1
    out_ref[core] = own_ref[...]
    out_ref[1 - core] = sib_ref[...]


def weight_place_kernel(me_ref, *refs):
    out_ref = refs[-1]
    per = refs[0].shape[1]
    for e, r in enumerate(refs[:-1]):
        for q in range(2):
            row = (((me_ref[0] >> 1) ^ e) << 1) + q
            out_ref[pl.ds(pl.multiple_of(row * per, per), per), :] = r[q]


def dense_kernel(n_col, me_ref, wt_ref, w_ref, *refs):
    s_refs, g_refs = refs[:n_col][::-1], refs[n_col : 2 * n_col][::-1]
    o_refs, y_refs = refs[2 * n_col : 3 * n_col], refs[3 * n_col : 4 * n_col]
    sz_ref = refs[4 * n_col]
    f_loc = s_refs[0].shape[0]
    n_f = f_loc * n_col
    s_ref, z_ref = sz_ref.at[pl.ds(0, n_f)], sz_ref.at[pl.ds(n_f, sz_ref.shape[0] - n_f)]
    me = me_ref[0]
    for k in range(n_col):
        s_ref[pl.ds(pl.multiple_of((me ^ k) * f_loc, f_loc), f_loc), :] = s_refs[k][...]
    s_all = s_ref[...]
    for k in range(n_col):
        rows = pl.ds(pl.multiple_of((me ^ k) * f_loc, f_loc), f_loc)
        pre = jnp.dot(wt_ref[rows, :], s_all, preferred_element_type=F32)
        sig = 1.0 / (1.0 + jnp.exp(-pre))
        o_refs[k][...] = (pre * sig).astype(BF)
        slope = sig * (1.0 + pre * (1.0 - sig))
        z_ref[rows, :] = (g_refs[k][...].astype(F32) * slope).astype(BF)
    z_all = z_ref[...]
    for k in range(n_col):
        rows = pl.ds(pl.multiple_of((me ^ k) * f_loc, f_loc), f_loc)
        y_refs[k][...] = jnp.dot(w_ref[rows, :], z_all, preferred_element_type=F32).astype(BF)


def gather_blocks(wide_ref, me, refs):
    width = refs[0].shape[1]
    for k, r in enumerate(refs):
        wide_ref[:, pl.ds(pl.multiple_of((me ^ k) * width, width), width)] = r[...]


def place_kernel(me_ref, *refs):
    wide_ref = refs[-1]
    width = refs[0].shape[1]
    parts = [refs[0], *refs[-2:0:-1]]
    for k, r in enumerate(parts):
        at = pl.multiple_of((me_ref[0] ^ k) * width, width)
        wide_ref[:, pl.ds(at, width)] = r[: wide_ref.shape[0], :]


def turn_kernel(x_ref, out_ref):
    out_ref[...] = x_ref[...].T


def split_kernel(me_ref, x_ref, *outs):
    width = outs[0].shape[1]
    for k, out in enumerate(outs):
        out[...] = x_ref[:, pl.ds(pl.multiple_of((me_ref[0] ^ k) * width, width), width)]


def weight_cols_kernel(n_chip, me_ref, *refs):
    n_col = (len(refs) - n_chip - 2) // 2
    ins, o_refs = refs[:n_chip], refs[n_chip : n_chip + n_col]
    outs, own_ref, sum_ref = refs[n_chip + n_col : -2], refs[-2], refs[-1]
    total = ins[0][...]
    for r in ins[1:]:
        total += r[...].astype(F32)
    sum_ref[...] = total
    h_loc, part = o_refs[0].shape
    rows = total.shape[0] * h_loc // part
    for k, out in enumerate(outs):
        if k:
            out[:h_loc, :] = o_refs[k][...]
        for c in range(n_col):

            @pl.when(me_ref[0] ^ k == c)
            def _():
                mine = sum_ref[:, c * h_loc : (c + 1) * h_loc]
                if k == 0:
                    own_ref[...] = mine
                else:
                    for i in range(part // h_loc):
                        out[h_loc : h_loc + rows, i * h_loc : (i + 1) * h_loc] = mine[
                            i * rows : (i + 1) * rows
                        ].astype(BF)


def weight_scale_kernel(scale, own_ref, *refs):
    out_ref = refs[-1]
    n_rows, h_loc = own_ref.shape
    rows = n_rows * h_loc // refs[0].shape[1]
    for i in range(n_rows // rows):
        total = own_ref[i * rows : (i + 1) * rows, :]
        for r in refs[:-1]:
            total += r[h_loc : h_loc + rows, i * h_loc : (i + 1) * h_loc].astype(F32)
        out_ref[i * rows : (i + 1) * rows, :] = total * scale


def shards(features, weight, tile_cols, tile_rows, tile_count, tile_values, out_grad):
    n_row, n_col = lax.axis_size("row"), lax.axis_size("col")
    n_chip = n_row // 2
    me_r, me_c = lax.axis_index("row").astype(jnp.int32), lax.axis_index("col").astype(jnp.int32)
    mer, mec = me_r.reshape(1), me_c.reshape(1)
    f_loc, nodes = features.shape
    h_loc = out_grad.shape[0]
    n_f, n_h = weight.shape
    row_tiles = nodes // TILE
    part = nodes // n_col
    slots = tile_cols.shape[1]
    per = 2 * SLOT
    sds = jax.ShapeDtypeStruct
    tile_flops = 2 * f_loc * TILE * TILE
    tile_bytes = slots * TILE * TILE * 2

    def over_chips(x):
        return swap(x, "row", n_row, 1)

    sib_feat = over_chips(features)
    need = call(
        functools.partial(need_kernel, n_row, row_tiles),
        sds((n_row, 128), jnp.int32),
        [],
        (tile_count,),
        (tile_cols,),
    )
    mer, mec, need = lax.optimization_barrier((mer, mec, need))
    needs = [need] + [swap(need, "row", n_row, 2 * e) for e in range(1, n_chip)]
    length = -(-(slots + n_chip * per + 2 * UNROLL) // 128) * 128
    x_near = call(
        pack_kernel,
        sds((2 * row_tiles + 1, f_loc, TILE), BF),
        [],
        (mer,),
        (features, sib_feat),
        nbytes=f_loc * nodes * 8,
    )
    tile_values, mer, mec = lax.optimization_barrier((tile_values, mer, mec))
    tile_values = pl.pallas_call(
        load_kernel,
        out_shape=sds(tile_values.shape, BF),
        in_specs=[pl.BlockSpec(memory_space=pltpu.HBM)],
        out_specs=VM,
        scratch_shapes=[pltpu.SemaphoreType.DMA((LOADS,))],
        compiler_params=pltpu.CompilerParams(vmem_limit_bytes=24 << 20),
        cost_estimate=pl.CostEstimate(flops=0, bytes_accessed=tile_bytes, transcendentals=0),
    )(pltpu.with_memory_space_constraint(tile_values, pltpu.HBM))
    needs, x_near, tile_values = lax.optimization_barrier((needs, x_near, tile_values))
    sends = call(
        functools.partial(send_kernel, n_chip, row_tiles),
        [sds((per, f_loc, TILE), BF)] * (n_chip - 1),
        [],
        (mer, *needs[1:]),
        (x_near,),
        nbytes=4 * n_chip * per * f_loc * TILE,
    )
    got = [swap(x, "row", n_row, 2 * (e + 1)) for e, x in enumerate(sends)]
    needs, sends, lists_in, out_grad = lax.optimization_barrier(
        (needs, sends, (tile_cols, tile_rows), out_grad)
    )
    lists = call(
        functools.partial(lists_kernel, n_row, row_tiles),
        sds((8, length), jnp.int32),
        [],
        (tile_count, mer),
        lists_in,
    )
    table = jnp.concatenate(needs, axis=0)
    table = jnp.concatenate([table, over_chips(table)], axis=0)
    table = call(
        functools.partial(table_kernel, n_row), sds((n_row, 128), jnp.int32), [], (mer,), (table,)
    )
    got, table = lax.optimization_barrier((got, table))

    g_parts = call(
        split_kernel,
        [sds((h_loc, part), BF)] * n_col,
        [],
        (mec,),
        (out_grad,),
        nbytes=h_loc * nodes * 4,
    )
    grads = [g if k == 0 else swap(g, "col", n_col, k) for k, g in enumerate(g_parts)]

    acc = call(
        near_fwd_kernel,
        sds((row_tiles, f_loc, TILE), F32),
        [],
        (lists,),
        (x_near,),
        (tile_values,),
        flops=tile_flops * slots,
        nbytes=tile_bytes,
    )
    s_parts = call(
        functools.partial(far_fwd_kernel, n_chip - 1),
        [sds((f_loc, part), BF)] * n_col,
        [
            pltpu.VMEM(((n_chip - 1) * per + 1, f_loc, TILE), BF),
            pltpu.VMEM((row_tiles, f_loc, TILE), F32),
        ],
        (lists, mec),
        (*got[::-1], acc),
        (tile_values,),
        flops=tile_flops * slots,
        nbytes=tile_bytes,
    )
    s_got = [s if k == 0 else swap(s, "col", n_col, k) for k, s in enumerate(s_parts)]

    weight_t, _ = lax.optimization_barrier((weight, s_parts[0]))
    weight_t = call(turn_kernel, sds((n_h, n_f), BF), [], (), (weight_t,), nbytes=n_f * n_h * 4)
    res = call(
        functools.partial(dense_kernel, n_col),
        [sds((h_loc, part), BF)] * n_col
        + [sds((f_loc, part), BF)] * n_col
        + [sds((n_f + n_h, part), BF)],
        [],
        (mec,),
        (weight_t, weight, *s_got[::-1], *grads[::-1]),
        flops=4 * n_f * n_h * part,
        nbytes=n_f * part * 8,
    )
    o_parts, y_parts, sz = res[:n_col], res[n_col : 2 * n_col], res[-1]
    y_got = [y if k == 0 else swap(y, "col", n_col, k) for k, y in enumerate(y_parts)]

    w_rows = n_f // n_row
    w_parts = call(
        weight_kernel,
        [sds((w_rows, n_h), F32)] + [sds((w_rows, n_h), BF)] * (n_chip - 1),
        [],
        (mer,),
        (sz, over_chips(sz)),
        flops=2 * n_f * n_h * part,
        nbytes=n_f * part * 8,
    )
    w_chips = [w if e == 0 else swap(w, "row", n_row, 2 * e) for e, w in enumerate(w_parts)]
    more = -(-(w_rows * h_loc // part) // 16) * 16
    mixed = call(
        functools.partial(weight_cols_kernel, n_chip),
        [sds((h_loc + more, part), BF)] * n_col + [sds((w_rows, h_loc), F32)],
        [pltpu.VMEM((w_rows, n_h), F32)],
        (mec,),
        (w_chips[0], *w_chips[:0:-1], *o_parts),
        nbytes=n_h * part * 4,
    )
    w_own_cols = mixed[-1]
    mixed = [m if k == 0 else swap(m, "col", n_col, k) for k, m in enumerate(mixed[:-1])]

    y_got, _ = lax.optimization_barrier((y_got[::-1], w_chips[::-1]))
    back = call(
        functools.partial(far_bwd_kernel, n_col),
        [sds((f_loc, nodes), BF), sds((SLOT, f_loc, TILE), BF)]
        + [sds((per, f_loc, TILE), BF)] * (n_chip - 1),
        [
            pltpu.VMEM((row_tiles + 1, f_loc, TILE), BF),
            pltpu.VMEM((n_chip * per, f_loc, TILE), F32),
        ],
        (lists, mec, mer),
        tuple(y_got),
        (tile_values,),
        flops=tile_flops * slots,
        nbytes=tile_bytes,
    )
    y_wide, to_sib, contribs = back[0], back[1], back[2:]
    returned = [swap(x, "row", n_row, 2 * (e + 1)) for e, x in enumerate(contribs)]
    from_sib = over_chips(to_sib)

    w_mine = call(
        functools.partial(weight_scale_kernel, float(nodes * n_row) ** (-0.5)),
        sds((w_rows, h_loc), F32),
        [],
        (),
        (w_own_cols, *mixed[:0:-1]),
    )

    acc_b = call(
        own_bwd_kernel,
        sds((row_tiles, f_loc, TILE), F32),
        [pltpu.VMEM((row_tiles + 1, f_loc, TILE), BF)],
        (lists,),
        (y_wide,),
        (tile_values,),
        flops=tile_flops * slots,
        nbytes=tile_bytes,
    )
    returned, acc_b, w_mine = lax.optimization_barrier((returned[::-1], acc_b, w_mine))
    passed = call(
        forward_kernel,
        sds(((n_chip - 1) * SLOT, f_loc, TILE), BF),
        [],
        (mer,),
        tuple(returned),
    )
    output = call(
        place_kernel, sds((h_loc, nodes), BF), [], (mec,), (o_parts[0], *mixed[:0:-1]), nbytes=h_loc * nodes * 4
    )
    w_hop, output = lax.optimization_barrier((over_chips(w_mine), output))
    w_pair = call(pair_kernel, sds((2, w_rows, h_loc), F32), [], (mer,), (w_mine, w_hop))
    w_chips = [w_pair] + [swap(w_pair, "row", n_row, 2 * e) for e in range(1, n_chip)]

    input_grad = call(
        functools.partial(join_kernel, n_chip),
        sds((f_loc, nodes), BF),
        [pltpu.VMEM((row_tiles, f_loc, TILE), F32)],
        (mer, table),
        (acc_b, from_sib, over_chips(passed), *returned),
        nbytes=f_loc * nodes * 8,
    )
    w_chips, input_grad = lax.optimization_barrier((w_chips, input_grad))
    weight_grad = call(
        weight_place_kernel,
        sds((n_f, h_loc), F32),
        [],
        (mer,),
        tuple(w_chips),
        nbytes=n_f * h_loc * 8,
    )
    return output, input_grad, weight_grad


def solution(mesh):
    return jax.shard_map(
        shards,
        mesh=mesh,
        in_specs=(
            P("col", "row"),
            P(),
            P("row", None),
            P("row", None),
            P("row"),
            P("row", None, None),
            P("col", "row"),
        ),
        out_specs=(P("col", "row"), P("col", "row"), P(None, "col")),
        check_vma=False,
    )
```

```python
import functools

import jax
import jax.numpy as jnp
from jax import lax
from jax.experimental import pallas as pl
from jax.experimental.pallas import tpu as pltpu
from jax.sharding import PartitionSpec as P

TILE = 128
SLOT = 4
UNROLL = 16
LOADS = 8
BF = jnp.bfloat16
F32 = jnp.float32
VM = pl.BlockSpec(memory_space=pltpu.VMEM)
SM = pl.BlockSpec(memory_space=pltpu.SMEM)


def call(kernel, outs, scratch, smem, vmem, held=(), flops=0, nbytes=0, limit=24):
    return pl.pallas_call(
        kernel,
        out_shape=outs,
        in_specs=[SM] * len(smem) + [VM] * len(held) + [VM] * len(vmem),
        out_specs=jax.tree.map(lambda _: VM, outs),
        scratch_shapes=scratch,
        compiler_params=pltpu.CompilerParams(vmem_limit_bytes=limit << 20),
        cost_estimate=pl.CostEstimate(flops=flops, bytes_accessed=nbytes, transcendentals=0),
    )(*[pltpu.with_memory_space_constraint(x, pltpu.SMEM) for x in smem], *held, *vmem)


def swap(x, axis, n, k):
    return lax.ppermute(x, axis, [(i, i ^ k) for i in range(n)])


def flip(x, n):
    i = lax.broadcasted_iota(jnp.int32, (n, n), 0)
    j = lax.broadcasted_iota(jnp.int32, (n, n), 1)
    return jnp.sum(jnp.where(i == j, x, 0), axis=1 if x.shape[0] == 1 else 0, keepdims=True)


def iota(n, axis):
    return lax.broadcasted_iota(jnp.int32, (n, 1) if axis == 0 else (1, n), axis)


def ranks(cols, valid, blocks, row_tiles):
    b_col, b_row = iota(blocks, 0), iota(blocks, 1)
    hit = jnp.where((cols == b_col) & valid, 1, 0)
    used_col = jnp.max(hit, axis=1, keepdims=True)
    used_row = flip(used_col, blocks)
    same = (b_col // row_tiles) == (b_row // row_tiles)
    rank_row = jnp.sum(jnp.where(same & (b_col < b_row), used_col, 0), axis=0, keepdims=True)
    rank_col = jnp.sum(jnp.where(same & (b_row < b_col), used_row, 0), axis=1, keepdims=True)
    return used_row, rank_row, rank_col


def need_kernel(n_row, row_tiles, count_ref, cols_ref, need_ref):
    cols = cols_ref[...]
    blocks = n_row * row_tiles
    valid = iota(cols.shape[1], 1) < count_ref[0]
    used, rank, _ = ranks(cols, valid, blocks, row_tiles)
    b = iota(blocks, 1)
    owner = (b // row_tiles) == iota(n_row, 0)
    lane = iota(128, 1)
    total = jnp.zeros((n_row, 128), jnp.int32)
    for j in range(SLOT):
        pick = jnp.where((used > 0) & (rank == j), b % row_tiles, 0)
        total += jnp.where(
            lane == j, jnp.sum(jnp.where(owner, pick, 0), axis=1, keepdims=True), 0
        )
    need_ref[...] = total


def write_list(out_ref, which, key_row, key_col, valid_row, valid_col, groups, source, blank):
    slots, length = key_row.shape[1], out_ref.shape[1]
    t_row, t_col = iota(slots, 1), iota(slots, 0)
    key_row, key_col = jnp.where(valid_row, key_row, -1), jnp.where(valid_col, key_col, -1)
    g_col, g_row = iota(groups, 0), iota(128, 1)
    count = jnp.sum(jnp.where(key_row == g_col, 1, 0), axis=1, keepdims=True)
    even = ((count + 1) >> 1) << 1
    start = jnp.sum(jnp.where(g_col < g_row, even, 0), axis=0, keepdims=True)
    first = jnp.sum(jnp.where(key_col == g_row, start, 0), axis=1, keepdims=True)
    rank = jnp.sum(jnp.where((key_row == key_col) & (t_row < t_col), 1, 0), axis=1, keepdims=True)
    place = jnp.where(valid_col, first + rank, -1)
    word = t_col | (source << 10) | (key_col << 20)
    pad = blank << 10
    words = jnp.sum(jnp.where(place == iota(length, 1), word - pad, 0), axis=0, keepdims=True) + pad
    out_ref[which : which + 1, :] = words
    total = jnp.sum(even, axis=0, keepdims=True)
    steps = (total + (2 * UNROLL - 1)) // (2 * UNROLL)
    out_ref[4 + which : 5 + which, :] = jnp.broadcast_to(steps, (1, length))


def lists_kernel(n_row, row_tiles, count_ref, me_ref, cols_ref, rows_ref, out_ref):
    cols, rows = cols_ref[...], rows_ref[...]
    slots = cols.shape[1]
    blocks = n_row * row_tiles
    me, n_chip = me_ref[0], n_row // 2
    valid = iota(slots, 1) < count_ref[0]
    _, rank_row, rank_col = ranks(cols, valid, blocks, row_tiles)
    cols_c, rows_c = flip(cols, slots), flip(rows, slots)
    valid_c = iota(slots, 0) < count_ref[0]
    slot_c = jnp.sum(jnp.where(cols_c == iota(blocks, 1), rank_row, 0), axis=1, keepdims=True)
    slot_r = jnp.sum(jnp.where(cols == iota(blocks, 0), rank_col, 0), axis=0, keepdims=True)

    def away(c, s):
        owner = c // row_tiles
        return ((owner >> 1) ^ (me >> 1)) * (2 * SLOT) + (owner & 1) * SLOT + s

    away_r, away_c = away(cols, slot_r), away(cols_c, slot_c)
    per = 2 * SLOT
    chip, chip_c = cols // row_tiles >> 1 == me >> 1, cols_c // row_tiles >> 1 == me >> 1
    near, near_c = valid & chip, valid_c & chip_c
    far, far_c = valid & ~chip, valid_c & ~chip_c
    write_list(
        out_ref, 0, rows, rows_c, near, near_c, row_tiles, cols_c % (2 * row_tiles), 2 * row_tiles
    )
    write_list(
        out_ref, 1, rows, rows_c, far, far_c, row_tiles, away_c - per, (n_chip - 1) * per
    )
    own, own_c = valid & (cols // row_tiles == me), valid_c & (cols_c // row_tiles == me)
    other, other_c = valid & (cols // row_tiles != me), valid_c & (cols_c // row_tiles != me)
    write_list(out_ref, 2, away_r, away_c, other, other_c, n_chip * per, rows_c, row_tiles)
    write_list(
        out_ref, 3, cols % row_tiles, cols_c % row_tiles, own, own_c, row_tiles, rows_c, row_tiles
    )


def sparse_loop(list_ref, which, x_ref, tiles_ref, acc_ref, forward):
    def step(s, carry):
        for u in range(UNROLL):
            p = 2 * (s * UNROLL + u)
            w0 = list_ref[which, p]
            w1 = list_ref[which, p + 1]
            x = jnp.concatenate([x_ref[(w0 >> 10) & 1023], x_ref[(w1 >> 10) & 1023]], axis=1)
            t0, t1 = tiles_ref[w0 & 1023], tiles_ref[w1 & 1023]
            if forward:
                part = lax.dot_general(
                    x,
                    jnp.concatenate([t0, t1], axis=1),
                    (((1,), (1,)), ((), ())),
                    preferred_element_type=F32,
                )
            else:
                part = jnp.dot(x, jnp.concatenate([t0, t1], axis=0), preferred_element_type=F32)
            acc_ref[w0 >> 20] += part
        return carry

    lax.fori_loop(0, list_ref[4 + which, 0], step, 0)


def load_kernel(in_ref, after_ref, out_ref, sems):
    n = in_ref.shape[0] // LOADS
    copies = [
        pltpu.make_async_copy(
            in_ref.at[pl.ds(i * n, n)], out_ref.at[pl.ds(i * n, n)], sems.at[i]
        )
        for i in range(LOADS)
    ]
    for c in copies:
        c.start()
    for c in copies:
        c.wait()


def pack_kernel(me_ref, feat_ref, sib_ref, out_ref):
    tiles = feat_ref.shape[1] // TILE
    base = (me_ref[0] & 1) * tiles
    for k in range(tiles):
        out_ref[base + k] = feat_ref[:, k * TILE : (k + 1) * TILE]
        out_ref[tiles - base + k] = sib_ref[:, k * TILE : (k + 1) * TILE]
    out_ref[2 * tiles] = jnp.zeros_like(out_ref[0])


def send_kernel(n_chip, row_tiles, me_ref, *refs):
    need_refs, x_ref, outs = refs[: n_chip - 1], refs[n_chip - 1], refs[n_chip:]
    for need_ref, out in zip(need_refs, outs):
        for q in range(2):
            for j in range(SLOT):
                out[q * SLOT + j] = x_ref[
                    q * row_tiles + need_ref[((me_ref[0] >> 1) << 1) + q, j]
                ]


def fill_from_wide(x_ref, wide_ref, count):
    for k in range(count):
        x_ref[k] = wide_ref[:, k * TILE : (k + 1) * TILE]
    x_ref[count] = jnp.zeros_like(x_ref[count])


def near_fwd_kernel(list_ref, tiles_ref, x_ref, acc_ref):
    acc_ref[...] = jnp.zeros_like(acc_ref)
    sparse_loop(list_ref, 0, x_ref, tiles_ref, acc_ref, True)


def own_bwd_kernel(list_ref, tiles_ref, wide_ref, acc_ref, x_ref):
    fill_from_wide(x_ref, wide_ref, x_ref.shape[0] - 1)
    acc_ref[...] = jnp.zeros_like(acc_ref)
    sparse_loop(list_ref, 3, x_ref, tiles_ref, acc_ref, False)


def far_fwd_kernel(n_in, list_ref, me_ref, tiles_ref, *refs):
    ins, base_ref, rest = refs[:n_in][::-1], refs[n_in], refs[n_in + 1 :]
    outs, (x_ref, acc_ref) = rest[:-2], rest[-2:]
    per = 2 * SLOT
    for d, r in enumerate(ins):
        x_ref[d * per : (d + 1) * per] = r[...]
    x_ref[n_in * per] = jnp.zeros_like(x_ref[0])
    acc_ref[...] = base_ref[...]
    sparse_loop(list_ref, 1, x_ref, tiles_ref, acc_ref, True)
    per = acc_ref.shape[0] // len(outs)
    for k, out in enumerate(outs):
        block = me_ref[0] ^ k
        for i in range(per):
            out[:, i * TILE : (i + 1) * TILE] = acc_ref[block * per + i].astype(BF)


def weight_kernel(me_ref, own_ref, sib_ref, keep_ref, *outs):
    n_f = own_ref.shape[0] - keep_ref.shape[1]
    per = keep_ref.shape[0]
    core = me_ref[0] & 1
    pairs = [(r, r[n_f:, :]) for r in (own_ref, sib_ref)]
    for e in range(len(outs) + 1):
        row = ((((me_ref[0] >> 1) ^ e) << 1) + core) * per
        rows = pl.ds(pl.multiple_of(row, per), per)
        total = sum(
            lax.dot_general(r[rows, :], z, (((1,), (1,)), ((), ())), preferred_element_type=F32)
            for r, z in pairs
        )
        if e == 0:
            keep_ref[...] = total
        else:
            outs[e - 1][...] = total.astype(BF)


def far_bwd_kernel(n_col, list_ref, mec_ref, mer_ref, tiles_ref, *refs):
    ins, rest = refs[:n_col], refs[n_col:]
    wide_ref, sib_ref, (x_ref, acc_ref) = rest[0], rest[1], rest[-2:]
    outs = rest[2:-2]
    per = 2 * SLOT
    gather_blocks(wide_ref, mec_ref[0], ins[::-1])
    fill_from_wide(x_ref, wide_ref, x_ref.shape[0] - 1)
    acc_ref[...] = jnp.zeros_like(acc_ref)
    sparse_loop(list_ref, 2, x_ref, tiles_ref, acc_ref, False)
    for e, out in enumerate(outs):
        out[...] = acc_ref[(e + 1) * per : (e + 2) * per].astype(BF)
    other = 1 - (mer_ref[0] & 1)
    for j in range(SLOT):
        sib_ref[j] = acc_ref[other * SLOT + j].astype(BF)


def table_kernel(n_row, me_ref, all_ref, out_ref):
    for p in range(out_ref.shape[0]):
        out_ref[p : p + 1, :] = all_ref[pl.ds(p * n_row + me_ref[0], 1), :]


def forward_kernel(me_ref, *refs):
    other = 1 - (me_ref[0] & 1)
    for e, r in enumerate(refs[:-1][::-1]):
        for j in range(SLOT):
            refs[-1][e * SLOT + j] = r[other * SLOT + j]


def join_kernel(n_chip, me_ref, table_ref, base_ref, sib_ref, fwd_ref, *refs):
    ins, (out_ref, acc_ref) = refs[:-2][::-1], refs[-2:]
    core = me_ref[0] & 1

    def tile(e, j, other):
        return table_ref[other * n_chip + e, j]

    acc_ref[...] = base_ref[...]
    for j in range(SLOT):
        acc_ref[tile(0, j, 1)] += sib_ref[j].astype(F32)
        for e, r in enumerate(ins):
            acc_ref[tile(e + 1, j, 0)] += r[core * SLOT + j].astype(F32)
            acc_ref[tile(e + 1, j, 1)] += fwd_ref[e * SLOT + j].astype(F32)
    for k in range(acc_ref.shape[0]):
        out_ref[:, k * TILE : (k + 1) * TILE] = acc_ref[k].astype(BF)


def pair_kernel(me_ref, own_ref, sib_ref, out_ref):
    core = me_ref[0] & 1
    out_ref[core] = own_ref[...]
    out_ref[1 - core] = sib_ref[...]


def weight_place_kernel(me_ref, *refs):
    out_ref = refs[-1]
    per = refs[0].shape[1]
    for e, r in enumerate(refs[:-1]):
        for q in range(2):
            row = (((me_ref[0] >> 1) ^ e) << 1) + q
            out_ref[pl.ds(pl.multiple_of(row * per, per), per), :] = r[q]


def dense_kernel(n_col, me_ref, wt_ref, w_ref, *refs):
    s_refs, g_refs = refs[:n_col][::-1], refs[n_col : 2 * n_col][::-1]
    o_refs, y_refs = refs[2 * n_col : 3 * n_col], refs[3 * n_col : 4 * n_col]
    sz_ref = refs[4 * n_col]
    f_loc = s_refs[0].shape[0]
    n_f = f_loc * n_col
    s_ref, z_ref = sz_ref.at[pl.ds(0, n_f)], sz_ref.at[pl.ds(n_f, sz_ref.shape[0] - n_f)]
    me = me_ref[0]
    for k in range(n_col):
        s_ref[pl.ds(pl.multiple_of((me ^ k) * f_loc, f_loc), f_loc), :] = s_refs[k][...]
    s_all = s_ref[...]
    for k in range(n_col):
        rows = pl.ds(pl.multiple_of((me ^ k) * f_loc, f_loc), f_loc)
        pre = jnp.dot(wt_ref[rows, :], s_all, preferred_element_type=F32)
        sig = 1.0 / (1.0 + jnp.exp(-pre))
        o_refs[k][...] = (pre * sig).astype(BF)
        slope = sig * (1.0 + pre * (1.0 - sig))
        z_ref[rows, :] = (g_refs[k][...].astype(F32) * slope).astype(BF)
    z_all = z_ref[...]
    for k in range(n_col):
        rows = pl.ds(pl.multiple_of((me ^ k) * f_loc, f_loc), f_loc)
        y_refs[k][...] = jnp.dot(w_ref[rows, :], z_all, preferred_element_type=F32).astype(BF)


def gather_blocks(wide_ref, me, refs):
    width = refs[0].shape[1]
    for k, r in enumerate(refs):
        wide_ref[:, pl.ds(pl.multiple_of((me ^ k) * width, width), width)] = r[...]


def place_kernel(me_ref, *refs):
    wide_ref = refs[-1]
    width = refs[0].shape[1]
    parts = [refs[0], *refs[-2:0:-1]]
    for k, r in enumerate(parts):
        at = pl.multiple_of((me_ref[0] ^ k) * width, width)
        wide_ref[:, pl.ds(at, width)] = r[: wide_ref.shape[0], :]


def turn_kernel(x_ref, out_ref):
    out_ref[...] = x_ref[...].T


def split_kernel(me_ref, x_ref, *outs):
    width = outs[0].shape[1]
    for k, out in enumerate(outs):
        out[...] = x_ref[:, pl.ds(pl.multiple_of((me_ref[0] ^ k) * width, width), width)]


def weight_cols_kernel(n_chip, me_ref, *refs):
    n_col = (len(refs) - n_chip - 2) // 2
    ins, o_refs = refs[:n_chip], refs[n_chip : n_chip + n_col]
    outs, own_ref, sum_ref = refs[n_chip + n_col : -2], refs[-2], refs[-1]
    total = ins[0][...]
    for r in ins[1:]:
        total += r[...].astype(F32)
    sum_ref[...] = total
    h_loc, part = o_refs[0].shape
    rows = total.shape[0] * h_loc // part
    for k, out in enumerate(outs):
        if k:
            out[:h_loc, :] = o_refs[k][...]
        for c in range(n_col):

            @pl.when(me_ref[0] ^ k == c)
            def _():
                mine = sum_ref[:, c * h_loc : (c + 1) * h_loc]
                if k == 0:
                    own_ref[...] = mine
                else:
                    for i in range(part // h_loc):
                        out[h_loc : h_loc + rows, i * h_loc : (i + 1) * h_loc] = mine[
                            i * rows : (i + 1) * rows
                        ].astype(BF)


def weight_scale_kernel(scale, own_ref, *refs):
    out_ref = refs[-1]
    n_rows, h_loc = own_ref.shape
    rows = n_rows * h_loc // refs[0].shape[1]
    for i in range(n_rows // rows):
        total = own_ref[i * rows : (i + 1) * rows, :]
        for r in refs[:-1]:
            total += r[h_loc : h_loc + rows, i * h_loc : (i + 1) * h_loc].astype(F32)
        out_ref[i * rows : (i + 1) * rows, :] = total * scale


def shards(features, weight, tile_cols, tile_rows, tile_count, tile_values, out_grad):
    n_row, n_col = lax.axis_size("row"), lax.axis_size("col")
    n_chip = n_row // 2
    me_r, me_c = lax.axis_index("row").astype(jnp.int32), lax.axis_index("col").astype(jnp.int32)
    mer, mec = me_r.reshape(1), me_c.reshape(1)
    f_loc, nodes = features.shape
    h_loc = out_grad.shape[0]
    n_f, n_h = weight.shape
    row_tiles = nodes // TILE
    part = nodes // n_col
    slots = tile_cols.shape[1]
    per = 2 * SLOT
    sds = jax.ShapeDtypeStruct
    tile_flops = 2 * f_loc * TILE * TILE
    tile_bytes = slots * TILE * TILE * 2

    def over_chips(x):
        return swap(x, "row", n_row, 1)

    sib_feat = over_chips(features)
    need = call(
        functools.partial(need_kernel, n_row, row_tiles),
        sds((n_row, 128), jnp.int32),
        [],
        (tile_count,),
        (tile_cols,),
    )
    mer, mec, need = lax.optimization_barrier((mer, mec, need))
    needs = [need] + [swap(need, "row", n_row, 2 * e) for e in range(1, n_chip)]
    length = -(-(slots + n_chip * per + 2 * UNROLL) // 128) * 128
    x_near = call(
        pack_kernel,
        sds((2 * row_tiles + 1, f_loc, TILE), BF),
        [],
        (mer,),
        (features, sib_feat),
        nbytes=f_loc * nodes * 8,
    )
    needs, x_near, mer, mec = lax.optimization_barrier((needs, x_near, mer, mec))
    sends = call(
        functools.partial(send_kernel, n_chip, row_tiles),
        [sds((per, f_loc, TILE), BF)] * (n_chip - 1),
        [],
        (mer, *needs[1:]),
        (x_near,),
        nbytes=4 * n_chip * per * f_loc * TILE,
    )
    got = [swap(x, "row", n_row, 2 * (e + 1)) for e, x in enumerate(sends)]
    needs, sends, lists_in, out_grad = lax.optimization_barrier(
        (needs, sends, (tile_cols, tile_rows), out_grad)
    )
    lists = call(
        functools.partial(lists_kernel, n_row, row_tiles),
        sds((8, length), jnp.int32),
        [],
        (tile_count, mer),
        lists_in,
    )
    tile_values, sends = lax.optimization_barrier((tile_values, sends))
    tile_values = pl.pallas_call(
        load_kernel,
        out_shape=sds(tile_values.shape, BF),
        in_specs=[pl.BlockSpec(memory_space=pltpu.HBM), VM],
        out_specs=VM,
        scratch_shapes=[pltpu.SemaphoreType.DMA((LOADS,))],
        compiler_params=pltpu.CompilerParams(vmem_limit_bytes=24 << 20),
        cost_estimate=pl.CostEstimate(flops=0, bytes_accessed=tile_bytes, transcendentals=0),
    )(pltpu.with_memory_space_constraint(tile_values, pltpu.HBM), sends[0])
    table = jnp.concatenate(needs, axis=0)
    table = jnp.concatenate([table, over_chips(table)], axis=0)
    table = call(
        functools.partial(table_kernel, n_row), sds((n_row, 128), jnp.int32), [], (mer,), (table,)
    )
    got, table = lax.optimization_barrier((got, table))

    g_parts = call(
        split_kernel,
        [sds((h_loc, part), BF)] * n_col,
        [],
        (mec,),
        (out_grad,),
        nbytes=h_loc * nodes * 4,
    )
    grads = [g if k == 0 else swap(g, "col", n_col, k) for k, g in enumerate(g_parts)]

    acc = call(
        near_fwd_kernel,
        sds((row_tiles, f_loc, TILE), F32),
        [],
        (lists,),
        (x_near,),
        (tile_values,),
        flops=tile_flops * slots,
        nbytes=tile_bytes,
    )
    s_parts = call(
        functools.partial(far_fwd_kernel, n_chip - 1),
        [sds((f_loc, part), BF)] * n_col,
        [
            pltpu.VMEM(((n_chip - 1) * per + 1, f_loc, TILE), BF),
            pltpu.VMEM((row_tiles, f_loc, TILE), F32),
        ],
        (lists, mec),
        (*got[::-1], acc),
        (tile_values,),
        flops=tile_flops * slots,
        nbytes=tile_bytes,
    )
    s_got = [s if k == 0 else swap(s, "col", n_col, k) for k, s in enumerate(s_parts)]

    weight_t, _ = lax.optimization_barrier((weight, s_parts[0]))
    weight_t = call(turn_kernel, sds((n_h, n_f), BF), [], (), (weight_t,), nbytes=n_f * n_h * 4)
    res = call(
        functools.partial(dense_kernel, n_col),
        [sds((h_loc, part), BF)] * n_col
        + [sds((f_loc, part), BF)] * n_col
        + [sds((n_f + n_h, part), BF)],
        [],
        (mec,),
        (weight_t, weight, *s_got[::-1], *grads[::-1]),
        flops=4 * n_f * n_h * part,
        nbytes=n_f * part * 8,
    )
    o_parts, y_parts, sz = res[:n_col], res[n_col : 2 * n_col], res[-1]
    y_got = [y if k == 0 else swap(y, "col", n_col, k) for k, y in enumerate(y_parts)]

    w_rows = n_f // n_row
    w_parts = call(
        weight_kernel,
        [sds((w_rows, n_h), F32)] + [sds((w_rows, n_h), BF)] * (n_chip - 1),
        [],
        (mer,),
        (sz, over_chips(sz)),
        flops=2 * n_f * n_h * part,
        nbytes=n_f * part * 8,
    )
    w_chips = [w if e == 0 else swap(w, "row", n_row, 2 * e) for e, w in enumerate(w_parts)]
    more = -(-(w_rows * h_loc // part) // 16) * 16
    mixed = call(
        functools.partial(weight_cols_kernel, n_chip),
        [sds((h_loc + more, part), BF)] * n_col + [sds((w_rows, h_loc), F32)],
        [pltpu.VMEM((w_rows, n_h), F32)],
        (mec,),
        (w_chips[0], *w_chips[:0:-1], *o_parts),
        nbytes=n_h * part * 4,
    )
    w_own_cols = mixed[-1]
    mixed = [m if k == 0 else swap(m, "col", n_col, k) for k, m in enumerate(mixed[:-1])]

    y_got, _ = lax.optimization_barrier((y_got[::-1], w_chips[::-1]))
    back = call(
        functools.partial(far_bwd_kernel, n_col),
        [sds((f_loc, nodes), BF), sds((SLOT, f_loc, TILE), BF)]
        + [sds((per, f_loc, TILE), BF)] * (n_chip - 1),
        [
            pltpu.VMEM((row_tiles + 1, f_loc, TILE), BF),
            pltpu.VMEM((n_chip * per, f_loc, TILE), F32),
        ],
        (lists, mec, mer),
        tuple(y_got),
        (tile_values,),
        flops=tile_flops * slots,
        nbytes=tile_bytes,
    )
    y_wide, to_sib, contribs = back[0], back[1], back[2:]
    returned = [swap(x, "row", n_row, 2 * (e + 1)) for e, x in enumerate(contribs)]
    from_sib = over_chips(to_sib)

    w_mine = call(
        functools.partial(weight_scale_kernel, float(nodes * n_row) ** (-0.5)),
        sds((w_rows, h_loc), F32),
        [],
        (),
        (w_own_cols, *mixed[:0:-1]),
    )

    acc_b = call(
        own_bwd_kernel,
        sds((row_tiles, f_loc, TILE), F32),
        [pltpu.VMEM((row_tiles + 1, f_loc, TILE), BF)],
        (lists,),
        (y_wide,),
        (tile_values,),
        flops=tile_flops * slots,
        nbytes=tile_bytes,
    )
    returned, acc_b, w_mine = lax.optimization_barrier((returned[::-1], acc_b, w_mine))
    passed = call(
        forward_kernel,
        sds(((n_chip - 1) * SLOT, f_loc, TILE), BF),
        [],
        (mer,),
        tuple(returned),
    )
    output = call(
        place_kernel, sds((h_loc, nodes), BF), [], (mec,), (o_parts[0], *mixed[:0:-1]), nbytes=h_loc * nodes * 4
    )
    w_hop, output = lax.optimization_barrier((over_chips(w_mine), output))
    w_pair = call(pair_kernel, sds((2, w_rows, h_loc), F32), [], (mer,), (w_mine, w_hop))
    w_chips = [w_pair] + [swap(w_pair, "row", n_row, 2 * e) for e in range(1, n_chip)]

    input_grad = call(
        functools.partial(join_kernel, n_chip),
        sds((f_loc, nodes), BF),
        [pltpu.VMEM((row_tiles, f_loc, TILE), F32)],
        (mer, table),
        (acc_b, from_sib, over_chips(passed), *returned),
        nbytes=f_loc * nodes * 8,
    )
    w_chips, input_grad = lax.optimization_barrier((w_chips, input_grad))
    weight_grad = call(
        weight_place_kernel,
        sds((n_f, h_loc), F32),
        [],
        (mer,),
        tuple(w_chips),
        nbytes=n_f * h_loc * 8,
    )
    return output, input_grad, weight_grad


def solution(mesh):
    return jax.shard_map(
        shards,
        mesh=mesh,
        in_specs=(
            P("col", "row"),
            P(),
            P("row", None),
            P("row", None),
            P("row"),
            P("row", None, None),
            P("col", "row"),
        ),
        out_specs=(P("col", "row"), P("col", "row"), P(None, "col")),
        check_vma=False,
    )
```
